512 devices in a mesh: gx: 32 (over z, core), gy: 16 (over y, x).
Axes of the slice: x: 4, y: 4, z: 16, core: 2. Of those that a mesh axis runs over, the one named last changes fastest.
Arguments:
- patches: bfloat16 [512, 6144], P('gy', 'gx'), may hold values from -40 to 40
- ln_gain: float32 [6144], P('gx'), may hold values from 0.5 to 1.5
- weight_in: bfloat16 [6144, 24576], P('gx', 'gy'), may hold values from -0.12757759 to 0.12757759
- weight_out: bfloat16 [24576, 6144], P('gy', 'gx'), may hold values from -0.063788795 to 0.063788795
- upstream: bfloat16 [512, 6144], P('gy', 'gx'), may hold values from -18 to 18
- row_in: float32 [6144], P('gx'), may hold values from 7.68 to 92.16
- col_in: float32 [24576], P('gy'), may hold values from 7.68 to 92.16
- row_out: float32 [24576], P('gy'), may hold values from 7.68 to 92.16
- col_out: float32 [6144], P('gx'), may hold values from 7.68 to 92.16
Outputs:
- output: bfloat16 [512, 6144], P('gy', 'gx')
- input_grad: float32 [512, 6144], P('gy', 'gx')
- update_in: float32 [6144, 24576], P('gx', 'gy')
- update_out: float32 [24576, 6144], P('gy', 'gx')
The draws below stay inside these ranges and needn't reach their ends.
All inputs are finite; a program needn't handle non-finite values.
Results may differ from the reference program's by a relative error of at most 0.028.
Values may be sent and summed in bfloat16 or wider, within the bound.
A program may use at most 64 MiB of HBM per device.

```python
import math
import jax
import jax.numpy as jnp
from jax import lax

D = 6144
FF = 24576
ROWS = 512
N_GX = 32
N_GY = 16


def field_base(key, rows, cols):
    keys = jax.random.split(key, 1)
    base = jnp.clip(jax.random.normal(keys[0], (rows, cols), jnp.float32), -4.0, 4.0)
    return base


def scaled_field(key, rows, cols, row_low, row_high, noise_high):
    keys = jax.random.split(key, 3)
    base = field_base(keys[0], rows, cols)
    row_scale = jnp.exp(jax.random.uniform(keys[1], (rows, 1), jnp.float32, math.log(row_low), math.log(row_high)))
    rise = 3.0 ** (jnp.arange(cols, dtype=jnp.float32) / cols)
    noise = jnp.exp(jax.random.uniform(keys[2], (cols,), jnp.float32, 0.0, math.log(noise_high)))
    return base * row_scale * (rise * noise)[None, :]


def weight_field(key, rows, cols, fan_in, along_rows):
    keys = jax.random.split(key, 2)
    count = rows if along_rows else cols
    rise = 3.0 ** (jnp.arange(count, dtype=jnp.float32) / count - 0.5)
    noise = jnp.exp(jax.random.uniform(keys[1], (count,), jnp.float32, math.log(0.7), math.log(1.4)))
    factor = rise * noise / math.sqrt(fan_in)
    base = field_base(keys[0], rows, cols)
    if along_rows:
        return base * factor[:, None]
    return base * factor[None, :]


def rising_factor(key, count):
    noise = jnp.exp(jax.random.uniform(key, (count,), jnp.float32, math.log(0.5), math.log(2.0)))
    rise = 3.0 ** (jnp.arange(count, dtype=jnp.float32) / count)
    return ROWS * 0.03 * rise * noise


def draw_patches(key, part):
    return scaled_field(jax.random.fold_in(key, 11), ROWS, D, 0.1, 1.0, 3.3).astype(jnp.bfloat16)


def draw_upstream(key, part):
    return scaled_field(jax.random.fold_in(key, 12), ROWS, D, 0.3, 1.0, 1.5).astype(jnp.bfloat16)


def draw_weight_in(key, part):
    return weight_field(jax.random.fold_in(key, 13), D, FF, D, False).astype(jnp.bfloat16)


def draw_weight_out(key, part):
    return weight_field(jax.random.fold_in(key, 14), FF, D, FF, True).astype(jnp.bfloat16)


def draw_row_in(key, part):
    return rising_factor(jax.random.fold_in(key, 15), D)


def draw_col_in(key, part):
    return rising_factor(jax.random.fold_in(key, 16), FF)


def draw_row_out(key, part):
    return rising_factor(jax.random.fold_in(key, 17), FF)


def draw_col_out(key, part):
    return rising_factor(jax.random.fold_in(key, 18), D)


def setup_inputs(seed: int = 0) -> dict:
    seeds = jax.random.split(jax.random.key(seed), 10)
    return {
        "patches": draw_patches(jax.random.fold_in(seeds[9], 71), 0),
        "ln_gain": jnp.clip(1.0 + 0.1 * jax.random.normal(seeds[1], (D,), jnp.float32), 0.5, 1.5),
        "weight_in": draw_weight_in(jax.random.fold_in(seeds[9], 71), 0),
        "weight_out": draw_weight_out(jax.random.fold_in(seeds[9], 71), 0),
        "upstream": draw_upstream(jax.random.fold_in(seeds[9], 71), 0),
        "row_in": draw_row_in(jax.random.fold_in(seeds[9], 71), 0),
        "col_in": draw_col_in(jax.random.fold_in(seeds[9], 71), 0),
        "row_out": draw_row_out(jax.random.fold_in(seeds[9], 71), 0),
        "col_out": draw_col_out(jax.random.fold_in(seeds[9], 71), 0),
    }


def grouped_sum(left, right, groups, right_dim):
    rows = left.shape[0]
    width = left.shape[1] // groups
    lefts = left.reshape(rows, groups, width).transpose(1, 0, 2)
    if right_dim == 0:
        rights = right.reshape(groups, width, right.shape[1])
        dims = (((1,), (0,)), ((), ()))
        cols = right.shape[1]
    else:
        rights = right.reshape(right.shape[0], groups, width).transpose(1, 0, 2)
        dims = (((1,), (1,)), ((), ()))
        cols = right.shape[0]

    def accumulate(total, blocks):
        product = lax.dot_general(blocks[0], blocks[1], dims, preferred_element_type=jnp.float32)
        rounded = lax.optimization_barrier(product.astype(jnp.bfloat16))
        return (total + rounded.astype(jnp.float32), None)
    total, unused = lax.scan(accumulate, jnp.zeros((rows, cols), jnp.float32), (lefts, rights))
    return total

def rounded_once(values):
    return lax.optimization_barrier(values.astype(jnp.bfloat16)).astype(jnp.float32)

def factored(grad, row_prev, col_prev):
    squares = grad * grad + 1e-30
    row_new = 0.9 * row_prev + 0.1 * lax.optimization_barrier(jnp.mean(squares, axis=1))
    col_new = 0.9 * col_prev + 0.1 * lax.optimization_barrier(jnp.mean(squares, axis=0))
    scale = jnp.mean(row_new)
    return grad / jnp.sqrt(row_new[:, None] * col_new[None, :] / scale)

def reference(patches, ln_gain, weight_in, weight_out, upstream, row_in, col_in, row_out, col_out):
    x_float = patches.astype(jnp.float32)
    row_mean = lax.optimization_barrier(jnp.mean(x_float, axis=1, keepdims=True))
    row_var = lax.optimization_barrier(jnp.mean(x_float * x_float, axis=1, keepdims=True)) - row_mean * row_mean
    inv_std = lax.rsqrt(row_var + 1e-06)
    unit = (x_float - row_mean) * inv_std
    normed = (unit * ln_gain[None, :]).astype(jnp.bfloat16)
    hidden_pre = rounded_once(grouped_sum(normed, weight_in, N_GX, 0))
    phi = 0.5 * (1.0 + lax.erf(hidden_pre * 0.7071067811865476))
    hidden = (hidden_pre * phi).astype(jnp.bfloat16)
    branch = grouped_sum(hidden, weight_out, N_GY, 0)
    output = (x_float + branch).astype(jnp.bfloat16)
    hidden_grad = rounded_once(grouped_sum(upstream, weight_out, N_GX, 1))
    slope = phi + hidden_pre * jnp.exp(-0.5 * hidden_pre * hidden_pre) * 0.3989422804014327
    act_grad = (hidden_grad * slope).astype(jnp.bfloat16)
    grad_out = lax.dot_general(hidden, upstream, (((0,), (0,)), ((), ())), preferred_element_type=jnp.float32)
    grad_in = lax.dot_general(normed, act_grad, (((0,), (0,)), ((), ())), preferred_element_type=jnp.float32)
    normed_grad = grouped_sum(act_grad, weight_in, N_GY, 1)
    scaled = normed_grad * ln_gain[None, :]
    first_mean = lax.optimization_barrier(jnp.mean(scaled, axis=1, keepdims=True))
    second_mean = lax.optimization_barrier(jnp.mean(scaled * unit, axis=1, keepdims=True))
    input_grad = upstream.astype(jnp.float32) + inv_std * (scaled - first_mean - unit * second_mean)
    update_in = factored(grad_in, row_in, col_in)
    update_out = factored(grad_out, row_out, col_out)
    return (output, input_grad, update_in, update_out)
```

```python
import functools

import jax
import jax.numpy as jnp
from jax import lax
from jax.experimental import pallas as pl
from jax.experimental.pallas import tpu as pltpu
from jax.sharding import PartitionSpec as P

MESH = pl.DeviceIdType.MESH
F32 = jnp.float32
BF16 = jnp.bfloat16
SUBS = 2


def dot(a, b, ca, cb):
    return lax.dot_general(a, b, (((ca,), (cb,)), ((), ())), preferred_element_type=F32)


def aligned(i, n):
    return pl.multiple_of(i * n, n)


def kernel(
    n_gx, n_gy, d_model,
    patches, gain, upstream, w_in, w_out, row_in, row_out,
    output, input_grad, grad_in, grad_out, vec_f, vec_c, totals,
    up_all, nrm_all, wo_p, wi_p, hg_part, pre_part, hg_u, hg_d, pr_u, pr_d, full,
    unit_s, stat_m, stat_p, stat_z, br, ng, br_in, ng_in, ph1, ph1_in, fin_m, fin_p, fin_z,
    col_m, col_p, col_h, col_z, col_o,
    up_ss, up_rs, nr_ss, nr_rs, pt_ss, pt_rs, st_ss, st_rs, fi_ss, fi_rs, co_ss, co_rs,
    hu_ss, hu_rs, hd_ss, hd_rs, pu_ss, pu_rs, pd_ss, pd_rs,
    gu_ss, gu_rs, gd_ss, gd_rs, gp_ss, gp_rs, br_ss, br_rs, ng_ss, ng_rs, p1_ss, p1_rs,
):
    gx = lax.axis_index("gx")
    gy = lax.axis_index("gy")
    nz = n_gx // 2
    z = lax.div(gx, 2)
    core = lax.rem(gx, 2)
    other = 1 - core
    lin = gy * 2 + core
    n_lin = 2 * n_gy
    block, feats = patches.shape
    rows = block * n_gy
    cols = w_in.shape[1]
    half = cols // 2
    share = rows // nz
    ups, downs = nz // 2, nz - 1 - nz // 2

    def zdev(zz):
        return {"gx": zz * 2 + core, "gy": gy}

    partner = {"gx": z * 2 + other, "gy": gy}
    z_up = lax.rem(z + 1, nz)
    z_down = lax.rem(z + nz - 1, nz)

    def lindev(p):
        return {"gx": z * 2 + lax.rem(p, 2), "gy": lax.div(p, 2)}

    def remote(src, dst, ss, rs, dev):
        return pltpu.make_async_remote_copy(
            src_ref=src, dst_ref=dst, send_sem=ss, recv_sem=rs, device_id=dev, device_id_type=MESH
        )

    def each(lo, hi, f):
        def step(j, carry):
            f(j)
            return carry
        if lo < hi:
            lax.fori_loop(lo, hi, step, 0)

    barrier = pltpu.get_barrier_semaphore()

    def greet(dev):
        pl.semaphore_signal(barrier, inc=1, device_id=dev, device_id_type=MESH)

    each(1, nz, lambda j: greet(zdev(lax.rem(z + j, nz))))
    each(1, n_lin, lambda j: greet(lindev(lax.rem(lin + j, n_lin))))
    pl.semaphore_wait(barrier, nz - 1 + n_lin - 1)

    def plane_start(src, everything, ss, rs):
        def go(j):
            p = lax.rem(lin + j, n_lin)
            remote(src, everything.at[core, pl.ds(aligned(gy, block), block)], ss.at[j], rs.at[lin], lindev(p)).start()
        each(1, n_lin, go)

    def plane_wait(src, everything, ss, rs):
        def done(j):
            p = lax.rem(lin + j, n_lin)
            landed = everything.at[lax.rem(p, 2), pl.ds(aligned(lax.div(p, 2), block), block)]
            copy = remote(src, landed, ss.at[j], rs.at[p], lindev(p))
            copy.wait_send()
            copy.wait_recv()
        each(1, n_lin, done)

    def chips_start(src, slots, ss, rs):
        def go(j):
            zz = lax.rem(z + j, nz)
            remote(src, slots.at[z], ss.at[j], rs.at[z], zdev(zz)).start()
        each(1, nz, go)

    def chips_wait(src, slots, ss, rs):
        def done(j):
            zz = lax.rem(z + j, nz)
            copy = remote(src, slots.at[zz], ss.at[j], rs.at[zz], zdev(zz))
            copy.wait_send()
            copy.wait_recv()
        each(1, nz, done)

    def scatter_start(src, slots, ss, rs, whole):
        def go(j):
            g = lax.rem(gy + j, n_gy)
            part = src if whole else src.at[pl.ds(aligned(g, block), block)]
            remote(part, slots.at[gy], ss.at[j], rs.at[gy], {"gx": gx, "gy": g}).start()
        each(1, n_gy, go)

    def scatter_wait(src, slots, ss, rs, whole):
        def done(j):
            g = lax.rem(gy + j, n_gy)
            part = src if whole else src.at[pl.ds(aligned(g, block), block)]
            copy = remote(part, slots.at[g], ss.at[j], rs.at[g], {"gx": gx, "gy": g})
            copy.wait_send()
            copy.wait_recv()
        each(1, n_gy, done)

    def to_partner(src, dst, k):
        return remote(src, dst, pt_ss.at[k], pt_rs.at[k], partner)

    def across(first, second):
        lane = lax.broadcasted_iota(jnp.int32, (block, 128), 1)
        tile = jnp.where(lane == 0, first, jnp.where(lane == 1, second, 0.0))
        if block < 128:
            tile = jnp.concatenate([tile, jnp.zeros((128 - block, 128), F32)], axis=0)
        return jnp.transpose(tile)[:8]

    def back(message):
        tile = jnp.concatenate([message, jnp.zeros((120, 128), F32)], axis=0)
        tile = jnp.transpose(tile)
        return tile[:block, 0:1], tile[:block, 1:2]

    plane_start(upstream, up_all, up_ss, up_rs)
    send_wo = to_partner(w_out.at[pl.ds(aligned(other, half), half)], wo_p, 0)
    send_wo.start()
    send_wi = to_partner(w_in.at[:, pl.ds(aligned(other, half), half)], wi_p, 1)
    send_wi.start()
    x_float = patches[...].astype(F32)
    stat_m[...] = across(
        jnp.sum(x_float, axis=1, keepdims=True), jnp.sum(x_float * x_float, axis=1, keepdims=True)
    )
    send_st = to_partner(stat_m, stat_p, 2)
    send_st.start()
    up_all[core, pl.ds(aligned(gy, block), block), :] = upstream[...]
    send_st.wait()
    stat_z[z] = stat_m[...] + stat_p[...]
    chips_start(stat_z.at[z], stat_z, st_ss, st_rs)

    tile = 128 if rows % 128 == 0 else rows

    plane_wait(upstream, up_all, up_ss, up_rs)
    send_wo.wait()

    def hg_tile(i):
        r = pl.ds(aligned(i, tile), tile)
        mine = dot(up_all[core, r, :], w_out[pl.ds(aligned(core, half), half), :], 1, 1)
        hg_part[r, :] = mine + dot(up_all[other, r, :], wo_p[...], 1, 1)
    each(0, rows // tile, hg_tile)

    piece = share // SUBS

    def ring_step(s, part, buf, ss, rs, target, neighbour, first):
        for sub in range(SUBS):
            at = pl.ds(sub * piece, piece)
            own = part[pl.ds(pl.multiple_of(target * share + sub * piece, piece), piece), :]
            here = buf.at[s, at]
            there = buf.at[s + 1, at]
            copy = remote(here, there, ss.at[s, sub], rs.at[s + 1, sub], neighbour)
            if first:
                buf[s, at, :] = own.astype(BF16)
            else:
                remote(here, here, ss.at[s, sub], rs.at[s, sub], neighbour).wait_recv()
                buf[s, at, :] = (buf[s, at, :].astype(F32) + own).astype(BF16)
            copy.start()

    def reduce_step(kind, s, up=True, down=True, first=False):
        part, bu, bd, uss, urs, dss, drs = kind
        if up:
            ring_step(s, part, bu, uss, urs, lax.rem(z + ups - s + nz, nz), zdev(z_up), first)
        if down:
            ring_step(s, part, bd, dss, drs, lax.rem(z + nz - downs + s, nz), zdev(z_down), first)

    def reduce_end(kind):
        part, bu, bd, uss, urs, dss, drs = kind
        for sub in range(SUBS):
            at = pl.ds(sub * piece, piece)
            remote(bu.at[ups, at], bu.at[ups, at], uss.at[0, sub], urs.at[ups, sub], zdev(z_up)).wait_recv()
            remote(bd.at[downs, at], bd.at[downs, at], dss.at[0, sub], drs.at[downs, sub], zdev(z_down)).wait_recv()
        own = part[pl.ds(aligned(z, share), share), :]
        return (own + bu[ups].astype(F32)) + bd[downs].astype(F32)

    def reduce_sent(kind):
        part, bu, bd, uss, urs, dss, drs = kind

        def sent(buf, ss, rs, neighbour):
            def one(s):
                for sub in range(SUBS):
                    here = buf.at[s, pl.ds(sub * piece, piece)]
                    remote(here, here, ss.at[s, sub], rs.at[s, sub], neighbour).wait_send()
            return one
        each(0, ups, sent(bu, uss, urs, zdev(z_up)))
        each(0, downs, sent(bd, dss, drs, zdev(z_down)))

    hg = (hg_part, hg_u, hg_d, hu_ss, hu_rs, hd_ss, hd_rs)
    pre = (pre_part, pr_u, pr_d, pu_ss, pu_rs, pd_ss, pd_rs)
    reduce_step(hg, 0, first=True)

    chips_wait(stat_z.at[z], stat_z, st_ss, st_rs)
    total, squares = back(jnp.sum(stat_z[...], axis=0))
    row_mean = total / d_model
    row_var = squares / d_model - row_mean * row_mean
    inv_std = lax.rsqrt(row_var + 1e-06)
    unit = (patches[...].astype(F32) - row_mean) * inv_std
    unit_s[...] = unit
    mine = pl.ds(aligned(gy, block), block)
    nrm_all[core, mine, :] = (unit * gain[...]).astype(BF16)
    plane_start(nrm_all.at[core, mine], nrm_all, nr_ss, nr_rs)

    lag = min(2, downs)
    each(1, lag, lambda s: reduce_step(hg, s))
    plane_wait(nrm_all.at[core, mine], nrm_all, nr_ss, nr_rs)
    send_wi.wait()

    def pre_tile(i):
        r = pl.ds(aligned(i, tile), tile)
        own = dot(nrm_all[core, r, :], w_in[:, pl.ds(aligned(core, half), half)], 1, 0)
        pre_part[r, :] = own + dot(nrm_all[other, r, :], wi_p[...], 1, 0)
    each(0, rows // tile, pre_tile)
    reduce_step(pre, 0, first=True)
    joint = downs - lag

    def both(i):
        reduce_step(hg, lag + i)
        reduce_step(pre, 1 + i)
    each(0, joint, both)
    if ups > downs:
        reduce_step(hg, ups - 1, down=False)
    each(1 + joint, downs, lambda s: reduce_step(pre, s))
    if ups > downs:
        reduce_step(pre, ups - 1, down=False)

    hidden_grad = reduce_end(hg).astype(BF16).astype(F32)
    hidden_pre = reduce_end(pre).astype(BF16).astype(F32)
    phi = 0.5 * (1.0 + lax.erf(hidden_pre * 0.7071067811865476))
    slope = phi + hidden_pre * jnp.exp(-0.5 * hidden_pre * hidden_pre) * 0.3989422804014327
    own_rows = pl.ds(aligned(z, share), share)
    full[0, core, own_rows, :] = (hidden_pre * phi).astype(BF16)
    full[1, core, own_rows, :] = (hidden_grad * slope).astype(BF16)

    def rows_of(origin):
        return pl.ds(aligned(origin, share), share)

    def spread(k, origin, ss, rs, neighbour):
        ref = full.at[k, core, rows_of(origin)]
        return remote(ref, ref, ss, rs, neighbour)

    def hand_over(k, origin):
        return spread(k, origin, gp_ss.at[origin, k], gp_rs.at[origin, k], partner)

    def gather_up(s, k):
        return spread(k, lax.rem(z - s + nz, nz), gu_ss.at[s, k], gu_rs.at[s + 1, k], zdev(z_up))

    def gather_down(s, k):
        return spread(k, lax.rem(z + s, nz), gd_ss.at[s, k], gd_rs.at[s + 1, k], zdev(z_down))

    def gather_step(s, wait_up=True, wait_down=True, send_up=True, send_down=True):
        for k in range(2):
            if wait_up:
                origin = lax.rem(z - s + nz, nz)
                spread(k, origin, gu_ss.at[0, k], gu_rs.at[s, k], zdev(z_up)).wait_recv()
                if send_up:
                    gather_up(s, k).start()
                hand_over(k, origin).start()
            if wait_down:
                origin = lax.rem(z + s, nz)
                spread(k, origin, gd_ss.at[0, k], gd_rs.at[s, k], zdev(z_down)).wait_recv()
                if send_down:
                    gather_down(s, k).start()
                hand_over(k, origin).start()

    for k in range(2):
        gather_up(0, k).start()
        gather_down(0, k).start()
        hand_over(k, z).start()
    each(1, downs, lambda s: gather_step(s))
    gather_step(downs, send_up=ups > downs, send_down=False)
    if ups > downs:
        gather_step(ups, wait_down=False, send_up=False)

    def handed(o):
        for k in range(2):
            ref = full.at[k, other, rows_of(o)]
            copy = remote(ref, ref, gp_ss.at[o, k], gp_rs.at[o, k], partner)
            copy.wait_send()
            copy.wait_recv()
    each(0, nz, handed)

    def branch_tile(i):
        r = pl.ds(aligned(i, tile), tile)
        out = dot(full[0, 0, r, :], w_out[:half, :], 1, 0) + dot(full[0, 1, r, :], w_out[half:, :], 1, 0)
        br[r, :] = out.astype(BF16)
    each(0, rows // tile, branch_tile)
    scatter_start(br, br_in, br_ss, br_rs, False)

    def normed_tile(i):
        r = pl.ds(aligned(i, tile), tile)
        out = dot(full[1, 0, r, :], w_in[:, :half], 1, 1) + dot(full[1, 1, r, :], w_in[:, half:], 1, 1)
        ng[r, :] = out.astype(BF16)
    each(0, rows // tile, normed_tile)
    scatter_start(ng, ng_in, ng_ss, ng_rs, False)

    def rough(values):
        high = values.astype(BF16)
        return high, (values - high.astype(F32)).astype(BF16)

    nrm_t = jnp.transpose(nrm_all[core])
    ones_f = jnp.ones((8, feats), BF16)
    row_in_sum = jnp.zeros((8, feats), F32)
    col_out_sum = jnp.zeros((1, feats), F32)
    lines = lax.broadcasted_iota(jnp.int32, (8, half // 2), 0)
    packed = jnp.zeros((8, half // 2), F32)
    for h in range(2):
        gi = dot(nrm_t, full[1, h], 1, 0)
        grad_in[:, h * half:(h + 1) * half] = gi
        sq = gi * gi + 1e-30
        high, low = rough(sq)
        ones_h = jnp.ones((8, half), BF16)
        row_in_sum += dot(ones_h, high, 1, 1) + dot(ones_h, low, 1, 1)
        col = jnp.sum(sq, axis=0, keepdims=True)
        for q in range(2):
            packed = jnp.where(lines == 2 * h + q, col[:, q * (half // 2):(q + 1) * (half // 2)], packed)
        go = dot(full[0, h], up_all[core], 0, 0)
        grad_out[h * half:(h + 1) * half, :] = go
        sq = go * go + 1e-30
        high, low = rough(sq)
        col_out_sum += jnp.sum(sq, axis=0, keepdims=True)
        row = dot(ones_f, high, 1, 1) + dot(ones_f, low, 1, 1)
        for q in range(2):
            packed = jnp.where(lines == 4 + 2 * h + q, row[:, q * (half // 2):(q + 1) * (half // 2)], packed)
    col_m[...] = packed
    send_col = to_partner(col_m, col_p, 3)
    send_col.start()
    eight = lax.broadcasted_iota(jnp.int32, (8, feats), 0)
    row_out_total = jnp.sum(row_out[...], axis=1, keepdims=True)
    ph1[...] = jnp.where(
        eight == 0, row_in_sum, jnp.where(eight == 1, col_out_sum, jnp.broadcast_to(row_out_total, (8, feats)))
    )
    scatter_start(ph1, ph1_in, p1_ss, p1_rs, True)

    send_col.wait()
    chip_cols = col_m[...] + col_p[...]
    col_h[...] = jnp.where(core == 0, chip_cols[:4], chip_cols[4:])
    chips_start(col_h, col_z, co_ss, co_rs)

    scatter_wait(br, br_in, br_ss, br_rs, False)
    br_in[gy] = br[mine, :]
    branch = jnp.sum(br_in[...].astype(F32), axis=0)
    output[...] = (patches[...].astype(F32) + branch).astype(BF16)
    scatter_wait(ng, ng_in, ng_ss, ng_rs, False)
    ng_in[gy] = ng[mine, :]
    scaled = jnp.sum(ng_in[...].astype(F32), axis=0) * gain[...]
    unit = unit_s[...]
    message = across(jnp.sum(scaled, axis=1, keepdims=True), jnp.sum(scaled * unit, axis=1, keepdims=True))
    scatter_wait(ph1, ph1_in, p1_ss, p1_rs, True)
    ph1_in[gy] = ph1[...]
    sums = jnp.sum(ph1_in[...], axis=0)
    vec_f[...] = sums
    row_new = 0.9 * row_in[...] + 0.1 * (sums[0:1] / cols_total(cols, n_gy))
    lane8 = lax.broadcasted_iota(jnp.int32, (8, 128), 0)
    total_in = jnp.sum(row_new, axis=1, keepdims=True)
    total_out = jnp.sum(sums[1:2], axis=1, keepdims=True)
    fin_m[...] = jnp.where(lane8 == 2, total_in, jnp.where(lane8 == 3, total_out, message))
    send_fin = to_partner(fin_m, fin_p, 4)
    send_fin.start()
    send_fin.wait()
    fin_z[z] = fin_m[...] + fin_p[...]
    chips_start(fin_z.at[z], fin_z, fi_ss, fi_rs)
    chips_wait(col_h, col_z, co_ss, co_rs)
    col_z[z] = col_h[...]
    col_o[core] = jnp.sum(col_z[...], axis=0)
    send_out = to_partner(col_o.at[core], col_o.at[core], 5)
    send_out.start()
    reduce_sent(hg)
    reduce_sent(pre)

    def gathered(s):
        for k in range(2):
            gather_up(s, k).wait_send()
    each(0, ups, gathered)

    def gathered_down(s):
        for k in range(2):
            gather_down(s, k).wait_send()
    each(0, downs, gathered_down)
    chips_wait(fin_z.at[z], fin_z, fi_ss, fi_rs)
    final = jnp.sum(fin_z[...], axis=0)
    first_sum, second_sum = back(final)
    inv_std = lax.rsqrt(row_var + 1e-06)
    input_grad[...] = upstream[...].astype(F32) + inv_std * (
        scaled - first_sum / d_model - unit * (second_sum / d_model)
    )
    totals[...] = final
    send_out.wait_send()
    remote(col_o.at[core], col_o.at[other], pt_ss.at[5], pt_rs.at[5], partner).wait_recv()
    vec_c[...] = col_o[...]


def cols_total(cols, n_gy):
    return cols * n_gy


def exchange(n_gx, n_gy, d_model, args):
    patches, gain, upstream, w_in, w_out, row_in, row_out = args
    block, feats = patches.shape
    cols = w_in.shape[1]
    rows, half, nz = block * n_gy, cols // 2, n_gx // 2
    share = rows // nz
    ups, downs = nz // 2, nz - 1 - nz // 2
    vmem = pl.BlockSpec(memory_space=pltpu.VMEM)
    sems = lambda *shape: pltpu.SemaphoreType.DMA(shape)
    quarter = half // 2
    shapes = [
        ((2, rows, feats), BF16), ((2, rows, feats), BF16), ((half, feats), BF16), ((feats, half), BF16),
        ((rows, half), F32), ((rows, half), F32),
        ((ups + 1, share, half), BF16), ((downs + 1, share, half), BF16),
        ((ups + 1, share, half), BF16), ((downs + 1, share, half), BF16),
        ((2, 2, rows, half), BF16),
        ((block, feats), F32), ((8, 128), F32), ((8, 128), F32), ((nz, 8, 128), F32),
        ((rows, feats), BF16), ((rows, feats), BF16), ((n_gy, block, feats), BF16), ((n_gy, block, feats), BF16),
        ((8, feats), F32), ((n_gy, 8, feats), F32),
        ((8, 128), F32), ((8, 128), F32), ((nz, 8, 128), F32),
        ((8, quarter), F32), ((8, quarter), F32), ((4, quarter), F32), ((nz, 4, quarter), F32), ((2, 4, quarter), F32),
    ]
    lin = 2 * n_gy
    semaphores = [
        sems(lin), sems(lin), sems(lin), sems(lin), sems(6), sems(6),
        sems(nz), sems(nz), sems(nz), sems(nz), sems(nz), sems(nz),
        sems(ups, SUBS), sems(ups + 1, SUBS), sems(downs, SUBS), sems(downs + 1, SUBS),
        sems(ups, SUBS), sems(ups + 1, SUBS), sems(downs, SUBS), sems(downs + 1, SUBS),
        sems(ups, 2), sems(ups + 1, 2), sems(downs, 2), sems(downs + 1, 2), sems(nz, 2), sems(nz, 2),
        sems(n_gy), sems(n_gy), sems(n_gy), sems(n_gy), sems(n_gy), sems(n_gy),
    ]
    outs = [
        jax.ShapeDtypeStruct((block, feats), BF16), jax.ShapeDtypeStruct((block, feats), F32),
        jax.ShapeDtypeStruct((feats, cols), F32), jax.ShapeDtypeStruct((cols, feats), F32),
        jax.ShapeDtypeStruct((8, feats), F32), jax.ShapeDtypeStruct((2, 4, quarter), F32),
        jax.ShapeDtypeStruct((8, 128), F32),
    ]
    return pl.pallas_call(
        functools.partial(kernel, n_gx, n_gy, d_model),
        out_shape=outs,
        in_specs=[vmem] * 7,
        out_specs=[vmem] * 7,
        scratch_shapes=[pltpu.VMEM(s, t) for s, t in shapes] + semaphores,
        compiler_params=pltpu.CompilerParams(
            collective_id=0, has_side_effects=True, vmem_limit_bytes=48 * 1024 * 1024
        ),
        name="block_step",
    )(*args)


def solution(mesh):
    n_gx, n_gy = mesh.shape["gx"], mesh.shape["gy"]

    def body(patches, ln_gain, weight_in, weight_out, upstream, row_in, col_in, row_out, col_out):
        feats, cols = weight_in.shape
        d_model, ff = feats * n_gx, cols * n_gy
        output, input_grad, grad_in, grad_out, vec_f, vec_c, totals = exchange(
            n_gx, n_gy, d_model,
            (patches, ln_gain[None], upstream, weight_in, weight_out, row_in[None], row_out[None]),
        )
        row_in_new = 0.9 * row_in + 0.1 * (vec_f[0] / ff)
        col_out_new = 0.9 * col_out + 0.1 * (vec_f[1] / ff)
        col_in_new = 0.9 * col_in + 0.1 * (vec_c[0].reshape(-1) / d_model)
        row_out_new = 0.9 * row_out + 0.1 * (vec_c[1].reshape(-1) / d_model)
        mean_in = totals[2, 0] / d_model
        mean_out = 0.9 * (vec_f[2, 0] / ff) + 0.1 * (totals[3, 0] / d_model / ff)
        update_in = grad_in / jnp.sqrt(row_in_new[:, None] * col_in_new[None, :] / mean_in)
        update_out = grad_out / jnp.sqrt(row_out_new[:, None] * col_out_new[None, :] / mean_out)
        return output, input_grad, update_in, update_out

    return jax.shard_map(
        body,
        mesh=mesh,
        in_specs=(
            P("gy", "gx"), P("gx"), P("gx", "gy"), P("gy", "gx"), P("gy", "gx"), P("gx"), P("gy"), P("gy"), P("gx"),
        ),
        out_specs=(P("gy", "gx"), P("gy", "gx"), P("gx", "gy"), P("gy", "gx")),
        check_vma=False,
    )
```

```python
import functools

import jax
import jax.numpy as jnp
from jax import lax
from jax.experimental import pallas as pl
from jax.experimental.pallas import tpu as pltpu
from jax.sharding import PartitionSpec as P

MESH = pl.DeviceIdType.MESH
F32 = jnp.float32
BF16 = jnp.bfloat16
SUBS = 4
GSUBS = 2
LAG = 3


def dot(a, b, ca, cb):
    return lax.dot_general(a, b, (((ca,), (cb,)), ((), ())), preferred_element_type=F32)


def aligned(i, n):
    return pl.multiple_of(i * n, n)


def plane_offsets(n_gy):
    side = next(k for k in range(int(n_gy ** 0.5), 0, -1) if n_gy % k == 0)
    wide = n_gy // side

    def hops(dy, dx):
        return min(dy, side - dy) + min(dx, wide - dx)

    offsets = [(dy, dx) for dy in range(side) for dx in range(wide) if dy or dx]
    return side, wide, sorted(offsets, key=lambda o: hops(*o))


def kernel(
    n_gx, n_gy, d_model,
    patches_h, gain_h, upstream_h, w_in_h, w_out_h, row_in_h, col_out_h, col_in_h, row_out_h,
    output, input_grad, grad_in, grad_out, totals,
    patches, gain, upstream, w_in, w_out, row_in, col_out, col_in, row_out,
    up_all, x_all, nrm_all, wo_p, wi_p, gains, hg_part, pre_part, hg_buf, pre_buf, hg_x, pre_x, full,
    unit_s, stat_m, stat_p, stat_z, means, br, ng, br_in, ng_in, ph1, ph1_in, fin_z,
    col_m, col_p, col_h, col_z, col_o,
    ld, up_ss, up_rs, uf_ss, uf_rs, xs_ss, xs_rs, xf_ss, xf_rs, pt_ss, pt_rs, st_ss, st_rs, fi_ss, fi_rs, co_ss, co_rs,
    ms_ss, ms_rs, hr_ss, hr_rs, pr_ss, pr_rs, hx_ss, hx_rs, px_ss, px_rs,
    ga_ss, ga_rs, gp_ss, gp_rs, br_ss, br_rs, ng_ss, ng_rs, p1_ss, p1_rs,
):
    gx = lax.axis_index("gx")
    gy = lax.axis_index("gy")
    nz = n_gx // 2
    z = lax.div(gx, 2)
    core = lax.rem(gx, 2)
    other = 1 - core
    block, feats = patches.shape
    rows = block * n_gy
    cols = w_in.shape[1]
    ff = cols * n_gy
    half = cols // 2
    quarter = half // 2
    share = rows // nz
    far = nz // 2
    side, wide, offsets = plane_offsets(n_gy)
    gy_y, gy_x = lax.div(gy, wide), lax.rem(gy, wide)
    peers = [lax.rem(gy_y + dy, side) * wide + lax.rem(gy_x + dx, wide) for dy, dx in offsets]

    def zdev(zz):
        return {"gx": zz * 2 + core, "gy": gy}

    def pdev(g):
        return {"gx": gx, "gy": g}

    partner = {"gx": z * 2 + other, "gy": gy}
    turn = 1 - 2 * core

    def ahead(k):
        return lax.rem(z + turn * k + nz, nz)

    def behind(k):
        return lax.rem(z - turn * k + nz, nz)

    next_dev = zdev(ahead(1))

    def remote(src, dst, ss, rs, dev):
        return pltpu.make_async_remote_copy(
            src_ref=src, dst_ref=dst, send_sem=ss, recv_sem=rs, device_id=dev, device_id_type=MESH
        )

    def each(lo, hi, f):
        def step(j, carry):
            f(j)
            return carry
        if lo < hi:
            lax.fori_loop(lo, hi, step, 0)

    loads = [
        pltpu.make_async_copy(a, b, ld.at[k]) for k, (a, b) in enumerate((
            (upstream_h, upstream), (patches_h, patches), (w_out_h, w_out), (w_in_h, w_in),
            (gain_h, gain), (row_in_h, row_in), (col_out_h, col_out),
            (col_in_h, col_in), (row_out_h, row_out),
        ))
    ]
    for copy in loads:
        copy.start()

    barrier = pltpu.get_barrier_semaphore()

    def greet(dev):
        pl.semaphore_signal(barrier, inc=1, device_id=dev, device_id_type=MESH)

    each(1, n_gx, lambda j: greet({"gx": lax.rem(gx + j, n_gx), "gy": gy}))
    for g in peers:
        greet(pdev(g))
    x_float = None
    loads[1].wait()

    def across(first, second):
        lane = lax.broadcasted_iota(jnp.int32, (block, 128), 1)
        tile = jnp.where(lane == 0, first, jnp.where(lane == 1, second, 0.0))
        if block < 128:
            tile = jnp.concatenate([tile, jnp.zeros((128 - block, 128), F32)], axis=0)
        return jnp.transpose(tile)[:8]

    def back(message):
        tile = jnp.concatenate([message, jnp.zeros((128 - message.shape[0], 128), F32)], axis=0)
        tile = jnp.transpose(tile)
        return tile[:block, 0:1], tile[:block, 1:2]

    x_float = patches[...].astype(F32)
    stat_m[...] = across(
        jnp.sum(x_float, axis=1, keepdims=True), jnp.sum(x_float * x_float, axis=1, keepdims=True)
    )
    loads[0].wait()
    own_block = pl.ds(aligned(gy, block), block)
    up_all[core, own_block, :] = upstream[...]
    x_all[core, own_block, :] = patches[...]
    for copy in loads[2:]:
        copy.wait()
    gains[core] = gain[...]
    pl.semaphore_wait(barrier, n_gx - 1 + n_gy - 1)

    def to_partner(src, dst, k):
        return remote(src, dst, pt_ss.at[k], pt_rs.at[k], partner)

    def plane_start(src, everything, ss, rs, fs, fr):
        for k, g in enumerate(peers):
            remote(src, everything.at[core, own_block], ss.at[k], rs.at[gy], pdev(g)).start()
        remote(src, everything.at[core, own_block], fs.at[gy], fr.at[gy], partner).start()

    def plane_forward(src, everything, ss, rs, fs, fr):
        for k, g in enumerate(peers):
            landed = everything.at[core, pl.ds(aligned(g, block), block)]
            copy = remote(src, landed, ss.at[k], rs.at[g], pdev(g))
            copy.wait_recv()
            remote(landed, landed, fs.at[g], fr.at[g], partner).start()

    def plane_wait(src, everything, ss, rs, fs, fr):
        for k, g in enumerate(peers):
            remote(src, everything.at[core, own_block], ss.at[k], rs.at[g], pdev(g)).wait_send()

        def handed(g):
            landed = everything.at[other, pl.ds(aligned(g, block), block)]
            copy = remote(landed, landed, fs.at[g], fr.at[g], partner)
            copy.wait_send()
            copy.wait_recv()
        each(0, n_gy, handed)

    def chips_start(src, slots, ss, rs):
        def go(j):
            zz = lax.rem(z + j, nz)
            remote(src, slots.at[z], ss.at[j], rs.at[z], zdev(zz)).start()
        each(1, nz, go)

    def chips_wait(src, slots, ss, rs):
        def done(j):
            zz = lax.rem(z + j, nz)
            copy = remote(src, slots.at[zz], ss.at[j], rs.at[zz], zdev(zz))
            copy.wait_send()
            copy.wait_recv()
        each(1, nz, done)

    send_st = to_partner(stat_m, stat_p, 2)
    send_st.start()
    up = (upstream, up_all, up_ss, up_rs, uf_ss, uf_rs)
    plane_start(*up)
    send_wo = to_partner(w_out, wo_p, 0)
    send_wo.start()
    send_st.wait()
    stat_z[z] = stat_m[...] + stat_p[...]
    chips_start(stat_z.at[z], stat_z, st_ss, st_rs)
    xs = (patches, x_all, xs_ss, xs_rs, xf_ss, xf_rs)
    plane_start(*xs)
    send_wi = to_partner(w_in, wi_p, 1)
    send_wi.start()
    send_gain = to_partner(gains.at[core], gains.at[core], 5)
    send_gain.start()

    def rows_of(origin):
        return pl.ds(aligned(origin, share), share)

    def block_product(everything, own_weight, other_weight, t):
        r = rows_of(t)
        return dot(everything[core, r, :], own_weight, 1, 0) + dot(everything[other, r, :], other_weight, 1, 0)

    early = SUBS // 2
    strip_cols = cols // SUBS

    def sub_of(i):
        return lax.rem(i + core * early, SUBS)

    def prepare(kind, s):
        part, buf, ss, rs, everything, own_weight, other_weight, cross, xss, xrs = kind
        part[...] = block_product(everything, own_weight[...], other_weight[...], ahead(far - s))

    def reduce_step(kind, s):
        part, buf, ss, rs, everything, own_weight, other_weight, cross, xss, xrs = kind
        known = isinstance(s, int)
        for i in range(early if known and s == 0 else SUBS):
            sub = sub_of(i)
            own = part[:, pl.ds(pl.multiple_of(sub * strip_cols, 128), strip_cols)]
            here = buf.at[s, sub]
            if known and s == (0 if i < early else 1):
                buf[s, sub] = own.astype(BF16)
            else:
                remote(here, here, ss.at[s, sub], rs.at[s, sub], next_dev).wait_recv()
                buf[s, sub] = (buf[s, sub].astype(F32) + own).astype(BF16)
            remote(here, buf.at[s + 1, sub], ss.at[s, sub], rs.at[s + 1, sub], next_dev).start()

    def cross_copy(kind, i):
        part, buf, ss, rs, everything, own_weight, other_weight, cross, xss, xrs = kind
        return remote(buf.at[far, sub_of(early + i)], cross.at[i], xss.at[i], xrs.at[i], partner)

    def prepare_end(kind):
        part, buf, ss, rs, everything, own_weight, other_weight, cross, xss, xrs = kind
        mine = pl.ds(aligned(core, half), half)
        part[:, :half] = block_product(everything, own_weight[:, mine], other_weight[:, mine], z)

    def cross_start(kind):
        part, buf, ss, rs, everything, own_weight, other_weight, cross, xss, xrs = kind
        for i in range(early):
            sub = sub_of(early + i)
            remote(buf.at[far, sub], buf.at[far, sub], ss.at[0, sub], rs.at[far, sub], next_dev).wait_recv()
            cross_copy(kind, i).start()

    def reduce_end(kind, i):
        part, buf, ss, rs, everything, own_weight, other_weight, cross, xss, xrs = kind
        sub = sub_of(i)
        remote(buf.at[far, sub], buf.at[far, sub], ss.at[0, sub], rs.at[far, sub], next_dev).wait_recv()
        cross_copy(kind, i).wait_recv()
        own = part[:, i * strip_cols:(i + 1) * strip_cols]
        total = (own + buf[far, sub].astype(F32)) + cross[i].astype(F32)
        return total.astype(BF16).astype(F32)

    def reduce_sent(kind):
        part, buf, ss, rs, everything, own_weight, other_weight, cross, xss, xrs = kind

        def sent(s, count):
            for i in range(count):
                here = buf.at[s, sub_of(i)]
                remote(here, here, ss.at[s, sub_of(i)], rs.at[s, sub_of(i)], next_dev).wait_send()

        sent(0, early)
        each(1, far, lambda s: sent(s, SUBS))
        for i in range(early):
            cross_copy(kind, i).wait_send()

    hg = (hg_part, hg_buf, hr_ss, hr_rs, up_all, w_out, wo_p, hg_x, hx_ss, hx_rs)
    pre = (pre_part, pre_buf, pr_ss, pr_rs, nrm_all, w_in, wi_p, pre_x, px_ss, px_rs)

    plane_forward(*up)
    plane_wait(*up)
    send_wo.wait()
    prepare(hg, 0)
    reduce_step(hg, 0)
    prepare(hg, 1)

    chips_wait(stat_z.at[z], stat_z, st_ss, st_rs)
    stats = jnp.sum(stat_z[...], axis=0)
    row_mean = stats[0:1] / d_model
    row_var = stats[1:2] / d_model - row_mean * row_mean
    inv_row = lax.rsqrt(row_var + 1e-06)
    line8 = lax.broadcasted_iota(jnp.int32, (8, 128), 0)
    place = 2 * lax.rem(gy, 4)
    means[gy] = jnp.where(line8 == place, row_mean, jnp.where(line8 == place + 1, inv_row, 0.0))
    for k, g in enumerate(peers):
        remote(means.at[gy], means.at[gy], ms_ss.at[k], ms_rs.at[gy], pdev(g)).start()
    mean_own, inv_std = back(jnp.where(line8 == 0, row_mean, jnp.where(line8 == 1, inv_row, 0.0)))
    unit_s[...] = (patches[...].astype(F32) - mean_own) * inv_std
    plane_forward(*xs)
    reduce_step(hg, 1)
    lag = min(LAG, far)

    def hg_step(s):
        prepare(hg, s)
        reduce_step(hg, s)
    each(2, lag, hg_step)
    plane_wait(*xs)
    send_wi.wait()
    send_gain.wait_send()
    remote(gains.at[core], gains.at[other], pt_ss.at[5], pt_rs.at[5], partner).wait_recv()
    for k, g in enumerate(peers):
        copy = remote(means.at[gy], means.at[g], ms_ss.at[k], ms_rs.at[g], pdev(g))
        copy.wait_send()
        copy.wait_recv()
    tiles = [(means[4 * q] + means[4 * q + 1]) + (means[4 * q + 2] + means[4 * q + 3]) for q in range(n_gy // 4)]
    tiles.append(jnp.zeros((128 - 2 * n_gy, 128), F32))
    columns = jnp.transpose(jnp.concatenate(tiles, axis=0))
    for g in range(n_gy):
        r = slice(g * block, (g + 1) * block)
        for c in range(2):
            unit = (x_all[c, r, :].astype(F32) - columns[:block, 2 * g:2 * g + 1]) * columns[:block, 2 * g + 1:2 * g + 2]
            nrm_all[c, r, :] = (unit * gains[c]).astype(BF16)
    prepare(pre, 0)
    reduce_step(pre, 0)
    if lag < far:
        prepare(hg, lag)
    prepare(pre, 1)
    if lag < far:
        reduce_step(hg, lag)
    reduce_step(pre, 1)

    def both(i):
        prepare(hg, lag + 1 + i)
        prepare(pre, 2 + i)
        reduce_step(hg, lag + 1 + i)
        reduce_step(pre, 2 + i)
    joint = max(far - lag - 1, 0)
    each(0, joint, both)

    def pre_step(s):
        prepare(pre, s)
        reduce_step(pre, s)
    prepare_end(hg)
    cut_in = min(2 + joint, far - 1)
    each(2 + joint, far - 1, pre_step)
    if far - 1 >= 2 + joint:
        prepare(pre, far - 1)
        cross_start(hg)
        reduce_step(pre, far - 1)
    else:
        cross_start(hg)
    prepare_end(pre)
    cross_start(pre)
    for i in range(early):
        hidden_grad = reduce_end(hg, i)
        hidden_pre = reduce_end(pre, i)
        phi = 0.5 * (1.0 + lax.erf(hidden_pre * 0.7071067811865476))
        slope = phi + hidden_pre * jnp.exp(-0.5 * hidden_pre * hidden_pre) * 0.3989422804014327
        at = slice(i * strip_cols, (i + 1) * strip_cols)
        full[0, core, rows_of(z), at] = (hidden_pre * phi).astype(BF16)
        full[1, core, rows_of(z), at] = (hidden_grad * slope).astype(BF16)

    strip = share // GSUBS
    pieces = [(w, k, g) for w in range(2) for g in range(GSUBS) for k in range(2)]
    own_pieces, other_pieces = pieces[:len(pieces) // 2], pieces[len(pieces) // 2:]

    def spread(piece, origin, ss, rs, row, neighbour, to_row):
        w, k, g = piece
        h = core if w == 0 else other
        name = h * (2 * GSUBS) + g * 2 + k
        ref = full.at[k, h, pl.ds(pl.multiple_of(origin * share + g * strip, strip), strip)]
        return remote(ref, ref, ss.at[row, name], rs.at[to_row, name], neighbour)

    def ring_send(s, piece):
        return spread(piece, behind(s), ga_ss, ga_rs, s, next_dev, s + 1)

    def ring_arrival(s, piece):
        return spread(piece, behind(s), ga_ss, ga_rs, 0, next_dev, s)

    def hand_over(piece, origin):
        return spread(piece, origin, gp_ss, gp_rs, origin, partner, origin)

    def process(origins, first, awaited):
        def join(ref, *index):
            parts = [ref[(*index, rows_of(o), slice(None))] for o in origins]
            return parts[0] if len(parts) == 1 else jnp.concatenate(parts, axis=0)

        def arrive():
            for o, some in awaited:
                for piece in some:
                    hand_over(piece, o).wait_recv()

        def products(k):
            weight, out, slots, ss, rs = ((w_out, br, br_in, br_ss, br_rs), (w_in, ng, ng_in, ng_ss, ng_rs))[k]
            product = dot(join(full, k, 0), weight[:, :half], 1, 1) + dot(join(full, k, 1), weight[:, half:], 1, 1)
            product = product.astype(BF16)
            for i, o in enumerate(origins):
                out[rows_of(o), :] = product[i * share:(i + 1) * share]

                @pl.when(o != gy)
                def _():
                    remote(out.at[rows_of(o)], slots.at[gy], ss.at[o], rs.at[gy], pdev(o)).start()

        def gradient(k):
            left, grad = ((up_all, grad_out), (nrm_all, grad_in))[k]
            lhs = join(left, core)
            for h in range(2):
                at = slice(h * half, (h + 1) * half)
                term = dot(lhs, join(full, k, h), 0, 0)
                grad[:, at] = term if first else grad[:, at] + term

        def begin():
            arrive()
            products(0)

        return begin, lambda: products(1), lambda: gradient(0), lambda: gradient(1)

    def gather_step(s, forward, work):
        quarter_of = len(pieces) // 4
        for n, piece in enumerate(pieces):
            ring_arrival(s, piece).wait_recv()
            if piece in forward:
                ring_send(s, piece).start()
            hand_over(piece, behind(s)).start()
            if (n + 1) % quarter_of == 0:
                work[n // quarter_of]()

    for piece in own_pieces:
        ring_send(0, piece).start()
        hand_over(piece, z).start()
    for piece in other_pieces:
        hand_over(piece, z).wait_recv()
        ring_send(0, piece).start()

    def pair(s):
        return (behind(s), ahead(s)), False, ((ahead(s), pieces),)

    gather_step(1, pieces if far > 2 else own_pieces, process((z,), True, ()))
    if far > 2:
        each(2, far - 1, lambda s: gather_step(s, pieces, process(*pair(s - 1))))
        gather_step(far - 1, own_pieces, process(*pair(far - 2)))
    for work in process(*pair(far - 1)):
        work()
    for piece in own_pieces:
        ring_arrival(far, piece).wait_recv()
        hand_over(piece, behind(far)).start()
    for work in process((behind(far),), False, ((behind(far), other_pieces),)):
        work()

    def rough(values):
        high = values.astype(BF16)
        return high, (values - high.astype(F32)).astype(BF16)

    ones_h = jnp.ones((8, half), BF16)
    lines = lax.broadcasted_iota(jnp.int32, (8, quarter), 0)
    packed = jnp.zeros((8, quarter), F32)
    lane_sums = []
    for k, grad in enumerate((grad_in, grad_out)):
        lane_sum = jnp.zeros((8, feats), F32)
        for h in range(2):
            values = grad[:, h * half:(h + 1) * half]
            sq = values * values + 1e-30
            high, low = rough(sq)
            lane_sum += dot(ones_h, high, 1, 1) + dot(ones_h, low, 1, 1)
            col = jnp.sum(sq, axis=0, keepdims=True)
            for q in range(2):
                packed = jnp.where(lines == 4 * k + 2 * h + q, col[:, q * quarter:(q + 1) * quarter], packed)
        lane_sums.append(lane_sum)
    col_m[...] = packed
    send_col = to_partner(col_m, col_p, 3)
    send_col.start()
    eight = lax.broadcasted_iota(jnp.int32, (8, feats), 0)
    row_out_total = jnp.sum(jnp.sum(row_out[...], axis=0, keepdims=True), axis=1, keepdims=True)
    wide_feats = ph1.shape[1]
    message = jnp.where(
        eight == 0, lane_sums[0], jnp.where(eight == 1, lane_sums[1], jnp.broadcast_to(row_out_total, (8, feats)))
    )
    if wide_feats > feats:
        message = jnp.concatenate([message, jnp.zeros((8, wide_feats - feats), F32)], axis=1)
    ph1[...] = message
    for k, g in enumerate(peers):
        remote(ph1, ph1_in.at[gy], p1_ss.at[k], p1_rs.at[gy], pdev(g)).start()

    send_col.wait()
    chip_cols = col_m[...] + col_p[...]
    col_h[...] = jnp.where(core == 0, chip_cols[:4], chip_cols[4:])
    chips_start(col_h, col_z, co_ss, co_rs)

    def scattered(out, slots, ss, rs):
        for g in peers:
            copy = remote(out.at[rows_of(g)], slots.at[g], ss.at[g], rs.at[g], pdev(g))
            copy.wait_send()
            copy.wait_recv()
        slots[gy] = out[own_block, :]
        return jnp.sum(slots[...].astype(F32), axis=0)

    scaled = scattered(ng, ng_in, ng_ss, ng_rs) * gain[...]
    unit = unit_s[...]
    message = across(jnp.sum(scaled, axis=1, keepdims=True), jnp.sum(scaled * unit, axis=1, keepdims=True))[:4]
    for k, g in enumerate(peers):
        copy = remote(ph1, ph1_in.at[g], p1_ss.at[k], p1_rs.at[g], pdev(g))
        copy.wait_send()
        copy.wait_recv()
    ph1_in[gy] = ph1[...]
    sums = jnp.sum(ph1_in[...], axis=0)
    row_in_new = 0.9 * row_in[...] + 0.1 * (sums[0:1, :feats] / ff)
    col_out_new = 0.9 * col_out[...] + 0.1 * (sums[1:2, :feats] / ff)
    lane4 = lax.broadcasted_iota(jnp.int32, (4, 128), 0)
    total_in = jnp.sum(row_in_new, axis=1, keepdims=True)
    total_out = jnp.sum(sums[1:2, :feats], axis=1, keepdims=True)
    fin_z[gx] = jnp.where(lane4 == 2, total_in, jnp.where(lane4 == 3, total_out, message))

    def finish(j):
        return remote(fin_z.at[gx], fin_z.at[gx], fi_ss.at[j], fi_rs.at[gx], {"gx": lax.rem(gx + j, n_gx), "gy": gy})

    each(1, n_gx, lambda j: finish(j).start())
    output[...] = (patches[...].astype(F32) + scattered(br, br_in, br_ss, br_rs)).astype(BF16)

    pair = jnp.where(
        lax.broadcasted_iota(jnp.int32, (128, feats), 0) == 0, lax.rsqrt(row_in_new), lax.rsqrt(col_out_new)
    )
    if wide_feats > feats:
        pair = jnp.concatenate([pair, jnp.zeros((128, wide_feats - feats), F32)], axis=1)
    turned = [jnp.transpose(pair[:, i * 128:(i + 1) * 128]) for i in range(wide_feats // 128)]
    factors = (turned[0] if len(turned) == 1 else jnp.concatenate(turned, axis=0))[:feats]

    chips_wait(col_h, col_z, co_ss, co_rs)
    col_z[z] = col_h[...]
    col_o[core] = jnp.sum(col_z[...], axis=0)
    send_out = to_partner(col_o.at[core], col_o.at[core], 4)
    send_out.start()
    reduce_sent(hg)
    reduce_sent(pre)

    def ring_sent(s, some):
        for piece in some:
            ring_send(s, piece).wait_send()
    each(0, far - 1, lambda s: ring_sent(s, pieces))
    ring_sent(far - 1, own_pieces)

    def handed_over(o, some):
        for piece in some:
            hand_over(piece, o).wait_send()
    handed_over(z, own_pieces)
    each(1, far, lambda s: handed_over(behind(s), pieces))
    handed_over(behind(far), own_pieces)
    send_out.wait_send()
    remote(col_o.at[core], col_o.at[other], pt_ss.at[4], pt_rs.at[4], partner).wait_recv()
    lines = quarter // 128
    for k, (grad, before) in enumerate(((grad_in, col_in), (grad_out, row_out))):
        column_sums = col_o[k] / d_model
        for q in range(4):
            at = slice(q * quarter, (q + 1) * quarter)
            old = [before[q * lines + i:q * lines + i + 1, :] for i in range(lines)]
            old = old[0] if lines == 1 else jnp.concatenate(old, axis=1)
            column = lax.rsqrt(0.9 * old + 0.1 * column_sums[q:q + 1])
            grad[:, at] = grad[:, at] * (factors[:, k:k + 1] * column)

    def finished(j):
        copy = finish(j)
        copy.wait_send()
        source = lax.rem(gx + j, n_gx)
        remote(fin_z.at[gx], fin_z.at[source], fi_ss.at[j], fi_rs.at[source], {"gx": source, "gy": gy}).wait_recv()
    each(1, n_gx, finished)
    final = jnp.sum(fin_z[...], axis=0)
    first_sum, second_sum = back(final)
    input_grad[...] = upstream[...].astype(F32) + inv_std * (
        scaled - first_sum / d_model - unit * (second_sum / d_model)
    )
    mean_in = final[2:3] / d_model
    mean_out = 0.9 * (sums[2:3, :128] / ff) + 0.1 * (final[3:4] / d_model / ff)
    which = lax.broadcasted_iota(jnp.int32, (8, 128), 0)
    totals[...] = jnp.sqrt(jnp.where(which == 0, mean_in, mean_out))


def exchange(n_gx, n_gy, d_model, args):
    patches, gain, upstream, w_in, w_out, row_in, col_out, col_in, row_out = args
    block, feats = patches.shape
    cols = w_in.shape[1]
    rows, half, nz = block * n_gy, cols // 2, n_gx // 2
    share, far = rows // nz, nz // 2
    quarter = half // 2
    wide_feats = -(-feats // 128) * 128
    pieces = 4 * GSUBS
    strips = cols // SUBS
    early = SUBS // 2
    vmem = pl.BlockSpec(memory_space=pltpu.VMEM)
    hbm = pl.BlockSpec(memory_space=pltpu.HBM)
    shapes = [(a.shape, a.dtype) for a in args] + [
        ((2, rows, feats), BF16), ((2, rows, feats), BF16), ((2, rows, feats), BF16),
        ((feats, cols), BF16), ((feats, cols), BF16), ((2, 1, feats), F32),
        ((share, cols), F32), ((share, cols), F32),
        ((far + 1, SUBS, share, strips), BF16), ((far + 1, SUBS, share, strips), BF16),
        ((early, share, strips), BF16), ((early, share, strips), BF16),
        ((2, 2, rows, half), BF16),
        ((block, feats), F32), ((8, 128), F32), ((8, 128), F32), ((nz, 8, 128), F32), ((n_gy, 8, 128), F32),
        ((rows, feats), BF16), ((rows, feats), BF16), ((n_gy, block, feats), BF16), ((n_gy, block, feats), BF16),
        ((8, wide_feats), F32), ((n_gy, 8, wide_feats), F32), ((n_gx, 4, 128), F32),
        ((8, quarter), F32), ((8, quarter), F32), ((4, quarter), F32), ((nz, 4, quarter), F32), ((2, 4, quarter), F32),
    ]
    counts = [(9,)] + [(n_gy,)] * 8 + [(6,)] * 2 + [(nz,)] * 2 + [(n_gx,)] * 2 + [(nz,)] * 2
    counts += [(n_gy,)] * 2 + [(far, SUBS), (far + 1, SUBS)] * 2 + [(early,)] * 4
    counts += [(far, pieces), (far + 1, pieces)] + [(nz, pieces)] * 2 + [(n_gy,)] * 6
    outs = [
        jax.ShapeDtypeStruct((block, feats), BF16), jax.ShapeDtypeStruct((block, feats), F32),
        jax.ShapeDtypeStruct((feats, cols), F32), jax.ShapeDtypeStruct((feats, cols), F32),
        jax.ShapeDtypeStruct((8, 128), F32),
    ]
    return pl.pallas_call(
        functools.partial(kernel, n_gx, n_gy, d_model),
        out_shape=outs,
        in_specs=[hbm] * 9,
        out_specs=[vmem] * 5,
        scratch_shapes=[pltpu.VMEM(s, t) for s, t in shapes] + [pltpu.SemaphoreType.DMA(c) for c in counts],
        compiler_params=pltpu.CompilerParams(
            collective_id=0, has_side_effects=True, vmem_limit_bytes=48 * 1024 * 1024
        ),
        name="block_step",
    )(*(pltpu.with_memory_space_constraint(a, pltpu.HBM) for a in args))


def finish_kernel(
    output, input_grad, grad_in, grad_out, totals, output_h, input_grad_h, update_in_h, update_out_h, new_in, new_out, sems
):
    small = [
        pltpu.make_async_copy(output, output_h, sems.at[0]), pltpu.make_async_copy(input_grad, input_grad_h, sems.at[1])
    ]
    for copy in small:
        copy.start()
    half = grad_in.shape[1] // 2
    copies = []
    for k, (grad, new, target) in enumerate(((grad_in, new_in, update_in_h), (grad_out, new_out, update_out_h))):
        for h in range(2):
            at = slice(h * half, (h + 1) * half)
            new[:, at] = grad[:, at] * totals[k:k + 1, 0:1]
            part = pl.ds(h * half, half)
            copy = pltpu.make_async_copy(new.at[:, part], target.at[:, part], sems.at[2 + 2 * k + h])
            copy.start()
            copies.append(copy)
    for copy in small + copies:
        copy.wait()


def finish(output, input_grad, grad_in, grad_out, totals):
    vmem = pl.BlockSpec(memory_space=pltpu.VMEM)
    hbm = pl.BlockSpec(memory_space=pltpu.HBM)
    arrays = (output, input_grad, grad_in, grad_out)
    return pl.pallas_call(
        finish_kernel,
        out_shape=[jax.ShapeDtypeStruct(a.shape, a.dtype) for a in arrays],
        in_specs=[vmem] * 5,
        out_specs=[hbm] * 4,
        scratch_shapes=[
            pltpu.VMEM(grad_in.shape, F32), pltpu.VMEM(grad_out.shape, F32), pltpu.SemaphoreType.DMA((6,))
        ],
        compiler_params=pltpu.CompilerParams(vmem_limit_bytes=16 * 1024 * 1024),
        name="scale_updates",
    )(*arrays, totals)


def solution(mesh):
    n_gx, n_gy = mesh.shape["gx"], mesh.shape["gy"]

    def body(patches, ln_gain, weight_in, weight_out, upstream, row_in, col_in, row_out, col_out):
        d_model = weight_in.shape[0] * n_gx
        results = exchange(
            n_gx, n_gy, d_model,
            (
                patches, ln_gain[None], upstream, weight_in, weight_out.T, row_in[None], col_out[None],
                col_in.reshape(-1, 128), row_out.reshape(-1, 128),
            ),
        )
        output, input_grad, update_in, update_out = finish(*results)
        return output, input_grad, update_in, update_out.T

    return jax.shard_map(
        body,
        mesh=mesh,
        in_specs=(
            P("gy", "gx"), P("gx"), P("gx", "gy"), P("gy", "gx"), P("gy", "gx"), P("gx"), P("gy"), P("gy"), P("gx"),
        ),
        out_specs=(P("gy", "gx"), P("gy", "gx"), P("gx", "gy"), P("gy", "gx")),
        check_vma=False,
    )
```

```python
import functools

import jax
import jax.numpy as jnp
from jax import lax
from jax.experimental import pallas as pl
from jax.experimental.pallas import tpu as pltpu
from jax.sharding import PartitionSpec as P

MESH = pl.DeviceIdType.MESH
F32 = jnp.float32
BF16 = jnp.bfloat16
SUBS = 4
GSUBS = 2
LAG = 2


def dot(a, b, ca, cb):
    return lax.dot_general(a, b, (((ca,), (cb,)), ((), ())), preferred_element_type=F32)


def aligned(i, n):
    return pl.multiple_of(i * n, n)


def plane_offsets(n_gy):
    side = next(k for k in range(int(n_gy ** 0.5), 0, -1) if n_gy % k == 0)
    wide = n_gy // side

    def hops(dy, dx):
        return min(dy, side - dy) + min(dx, wide - dx)

    offsets = [(dy, dx) for dy in range(side) for dx in range(wide) if dy or dx]
    return side, wide, sorted(offsets, key=lambda o: hops(*o))


def kernel(
    n_gx, n_gy, d_model,
    patches_h, gain_h, upstream_h, w_in_h, w_out_h, row_in_h, col_out_h, col_in_h, row_out_h,
    output, input_grad, grad_in, grad_out, totals,
    patches, gain, upstream, w_in, w_out, row_in, col_out, col_in, row_out,
    up_all, x_all, nrm_all, wo_p, wi_p, gains, hg_part, pre_part, hg_buf, pre_buf, hg_x, pre_x, full,
    unit_s, stat_z, means, br, ng, br_in, ng_in, ph1, ph1_in, fin_z, sum_z, sum_p,
    col_m, col_p, col_h, col_z, col_o,
    ld, up_ss, up_rs, uf_ss, uf_rs, xs_ss, xs_rs, xf_ss, xf_rs, pt_ss, pt_rs, st_ss, st_rs, fi_ss, fi_rs, sz_ss, sz_rs, co_ss, co_rs, sp_ss, sp_rs,
    ms_ss, ms_rs, hr_ss, hr_rs, pr_ss, pr_rs, hx_ss, hx_rs, px_ss, px_rs,
    ga_ss, ga_rs, gp_ss, gp_rs, br_ss, br_rs, ng_ss, ng_rs, p1_ss, p1_rs,
):
    gx = lax.axis_index("gx")
    gy = lax.axis_index("gy")
    nz = n_gx // 2
    z = lax.div(gx, 2)
    core = lax.rem(gx, 2)
    other = 1 - core
    block, feats = patches.shape
    rows = block * n_gy
    cols = w_in.shape[1]
    ff = cols * n_gy
    half = cols // 2
    quarter = half // 2
    share = rows // nz
    far = nz // 2
    side, wide, offsets = plane_offsets(n_gy)
    gy_y, gy_x = lax.div(gy, wide), lax.rem(gy, wide)
    peers = [lax.rem(gy_y + dy, side) * wide + lax.rem(gy_x + dx, wide) for dy, dx in offsets]

    def zdev(zz):
        return {"gx": zz * 2 + core, "gy": gy}

    def pdev(g):
        return {"gx": gx, "gy": g}

    partner = {"gx": z * 2 + other, "gy": gy}
    turn = 1 - 2 * core

    def ahead(k):
        return lax.rem(z + turn * k + nz, nz)

    def behind(k):
        return lax.rem(z - turn * k + nz, nz)

    next_dev = zdev(ahead(1))

    def remote(src, dst, ss, rs, dev):
        return pltpu.make_async_remote_copy(
            src_ref=src, dst_ref=dst, send_sem=ss, recv_sem=rs, device_id=dev, device_id_type=MESH
        )

    def each(lo, hi, f):
        def step(j, carry):
            f(j)
            return carry
        if lo < hi:
            lax.fori_loop(lo, hi, step, 0)

    loads = [
        pltpu.make_async_copy(a, b, ld.at[k]) for k, (a, b) in enumerate((
            (upstream_h, upstream), (patches_h, patches), (w_out_h, w_out), (w_in_h, w_in),
            (gain_h, gain), (row_in_h, row_in), (col_out_h, col_out),
            (col_in_h, col_in), (row_out_h, row_out),
        ))
    ]
    for copy in loads:
        copy.start()

    barrier = pltpu.get_barrier_semaphore()

    def greet(dev):
        pl.semaphore_signal(barrier, inc=1, device_id=dev, device_id_type=MESH)

    each(1, n_gx, lambda j: greet({"gx": lax.rem(gx + j, n_gx), "gy": gy}))
    for g in peers:
        greet(pdev(g))
    x_float = None
    loads[1].wait()

    def across(first, second):
        lane = lax.broadcasted_iota(jnp.int32, (block, 128), 1)
        parts = [jnp.where(lane == 0, first, 0.0), jnp.where(lane == 0, second, 0.0)]
        if 2 * block < 128:
            parts.append(jnp.zeros((128 - 2 * block, 128), F32))
        return jnp.transpose(jnp.concatenate(parts, axis=0))[:1]

    def back(message):
        tile = jnp.transpose(jnp.broadcast_to(message, (128, 128)))
        return tile[:block, 0:1], tile[block:2 * block, 0:1]

    x_float = patches[...].astype(F32)
    stat_z[gx] = across(
        jnp.sum(x_float, axis=1, keepdims=True), jnp.sum(x_float * x_float, axis=1, keepdims=True)
    )
    loads[0].wait()
    own_block = pl.ds(aligned(gy, block), block)
    up_all[core, own_block, :] = upstream[...]
    x_all[core, own_block, :] = patches[...]
    for copy in loads[2:]:
        copy.wait()
    gains[core] = gain[...]
    pl.semaphore_wait(barrier, n_gx - 1 + n_gy - 1)

    def to_partner(src, dst, k):
        return remote(src, dst, pt_ss.at[k], pt_rs.at[k], partner)

    def plane_start(src, everything, ss, rs, fs, fr):
        for k, g in enumerate(peers):
            remote(src, everything.at[core, own_block], ss.at[k], rs.at[gy], pdev(g)).start()
        remote(src, everything.at[core, own_block], fs.at[gy], fr.at[gy], partner).start()

    def plane_forward(src, everything, ss, rs, fs, fr):
        for k, g in enumerate(peers):
            landed = everything.at[core, pl.ds(aligned(g, block), block)]
            copy = remote(src, landed, ss.at[k], rs.at[g], pdev(g))
            copy.wait_recv()
            remote(landed, landed, fs.at[g], fr.at[g], partner).start()

    def plane_wait(src, everything, ss, rs, fs, fr):
        for k, g in enumerate(peers):
            remote(src, everything.at[core, own_block], ss.at[k], rs.at[g], pdev(g)).wait_send()

        def handed(g):
            landed = everything.at[other, pl.ds(aligned(g, block), block)]
            copy = remote(landed, landed, fs.at[g], fr.at[g], partner)
            copy.wait_send()
            copy.wait_recv()
        each(0, n_gy, handed)

    def chips_start(src, slots, ss, rs):
        def go(j):
            zz = lax.rem(z + j, nz)
            remote(src, slots.at[z], ss.at[j], rs.at[z], zdev(zz)).start()
        each(1, nz, go)

    def chips_wait(src, slots, ss, rs):
        def done(j):
            zz = lax.rem(z + j, nz)
            copy = remote(src, slots.at[zz], ss.at[j], rs.at[zz], zdev(zz))
            copy.wait_send()
            copy.wait_recv()
        each(1, nz, done)

    def column_copy(slots, ss, rs, j, source):
        return remote(slots.at[gx], slots.at[source], ss.at[j], rs.at[source], {"gx": lax.rem(gx + j, n_gx), "gy": gy})

    def column_start(slots, ss, rs):
        each(1, n_gx, lambda j: column_copy(slots, ss, rs, j, gx).start())

    def column_wait(slots, ss, rs):
        def done(j):
            copy = column_copy(slots, ss, rs, j, lax.rem(gx + j, n_gx))
            copy.wait_send()
            copy.wait_recv()
        each(1, n_gx, done)

    def small_copy(slots, ss, rs, k, source):
        return remote(slots.at[gy], slots.at[source], ss.at[k], rs.at[source], pdev(peers[k]))

    def small_start(slots, ss, rs):
        for k in range(len(peers)):
            small_copy(slots, ss, rs, k, gy).start()

    def small_wait(slots, ss, rs):
        for k, g in enumerate(peers):
            copy = small_copy(slots, ss, rs, k, g)
            copy.wait_send()
            copy.wait_recv()

    stat = (stat_z, st_ss, st_rs)
    column_start(*stat)
    up = (upstream, up_all, up_ss, up_rs, uf_ss, uf_rs)
    plane_start(*up)
    send_wo = to_partner(w_out, wo_p, 0)
    send_wo.start()
    xs = (patches, x_all, xs_ss, xs_rs, xf_ss, xf_rs)
    plane_start(*xs)
    send_wi = to_partner(w_in, wi_p, 1)
    send_wi.start()
    send_gain = to_partner(gains.at[core], gains.at[core], 5)
    send_gain.start()

    def rows_of(origin):
        return pl.ds(aligned(origin, share), share)

    def block_product(everything, own_weight, other_weight, t):
        r = rows_of(t)
        return dot(everything[core, r, :], own_weight, 1, 0) + dot(everything[other, r, :], other_weight, 1, 0)

    early = SUBS // 2
    strip_cols = cols // SUBS

    def sub_of(i):
        return lax.rem(i + core * early, SUBS)

    def prepare(kind, s):
        part, buf, ss, rs, everything, own_weight, other_weight, cross, xss, xrs = kind
        part[...] = block_product(everything, own_weight[...], other_weight[...], ahead(far - s))

    def reduce_step(kind, s):
        part, buf, ss, rs, everything, own_weight, other_weight, cross, xss, xrs = kind
        known = isinstance(s, int)
        for i in range(early if known and s == 0 else SUBS):
            sub = sub_of(i)
            own = part[:, pl.ds(pl.multiple_of(sub * strip_cols, 128), strip_cols)]
            here = buf.at[s, sub]
            if known and s == (0 if i < early else 1):
                buf[s, sub] = own.astype(BF16)
            else:
                remote(here, here, ss.at[s, sub], rs.at[s, sub], next_dev).wait_recv()
                buf[s, sub] = (buf[s, sub].astype(F32) + own).astype(BF16)
            remote(here, buf.at[s + 1, sub], ss.at[s, sub], rs.at[s + 1, sub], next_dev).start()

    def cross_copy(kind, i):
        part, buf, ss, rs, everything, own_weight, other_weight, cross, xss, xrs = kind
        return remote(buf.at[far, sub_of(early + i)], cross.at[i], xss.at[i], xrs.at[i], partner)

    def prepare_end(kind):
        part, buf, ss, rs, everything, own_weight, other_weight, cross, xss, xrs = kind
        mine = pl.ds(aligned(core, half), half)
        part[:, :half] = block_product(everything, own_weight[:, mine], other_weight[:, mine], z)

    def cross_start(kind):
        part, buf, ss, rs, everything, own_weight, other_weight, cross, xss, xrs = kind
        for i in range(early):
            sub = sub_of(early + i)
            remote(buf.at[far, sub], buf.at[far, sub], ss.at[0, sub], rs.at[far, sub], next_dev).wait_recv()
            cross_copy(kind, i).start()

    def reduce_end(kind, i):
        part, buf, ss, rs, everything, own_weight, other_weight, cross, xss, xrs = kind
        sub = sub_of(i)
        remote(buf.at[far, sub], buf.at[far, sub], ss.at[0, sub], rs.at[far, sub], next_dev).wait_recv()
        cross_copy(kind, i).wait_recv()
        own = part[:, i * strip_cols:(i + 1) * strip_cols]
        total = (own + buf[far, sub].astype(F32)) + cross[i].astype(F32)
        return total.astype(BF16).astype(F32)

    def reduce_sent(kind):
        part, buf, ss, rs, everything, own_weight, other_weight, cross, xss, xrs = kind

        def sent(s, count):
            for i in range(count):
                here = buf.at[s, sub_of(i)]
                remote(here, here, ss.at[s, sub_of(i)], rs.at[s, sub_of(i)], next_dev).wait_send()

        sent(0, early)
        each(1, far, lambda s: sent(s, SUBS))
        for i in range(early):
            cross_copy(kind, i).wait_send()

    hg = (hg_part, hg_buf, hr_ss, hr_rs, up_all, w_out, wo_p, hg_x, hx_ss, hx_rs)
    pre = (pre_part, pre_buf, pr_ss, pr_rs, nrm_all, w_in, wi_p, pre_x, px_ss, px_rs)

    plane_forward(*up)
    column_wait(*stat)
    total, squares = back(jnp.sum(stat_z[...], axis=0))
    row_mean = total / d_model
    row_var = squares / d_model - row_mean * row_mean
    inv_std = lax.rsqrt(row_var + 1e-06)
    means[gy] = across(row_mean, inv_std)
    deviations = (means, ms_ss, ms_rs)
    small_start(*deviations)
    plane_wait(*up)
    send_wo.wait()
    prepare(hg, 0)
    reduce_step(hg, 0)
    prepare(hg, 1)

    unit_s[...] = (patches[...].astype(F32) - row_mean) * inv_std
    plane_forward(*xs)
    reduce_step(hg, 1)
    lag = min(LAG, far)

    def hg_step(s):
        prepare(hg, s)
        reduce_step(hg, s)
    each(2, lag, hg_step)
    plane_wait(*xs)
    send_wi.wait()
    send_gain.wait_send()
    remote(gains.at[core], gains.at[other], pt_ss.at[5], pt_rs.at[5], partner).wait_recv()
    small_wait(*deviations)
    lines = lax.broadcasted_iota(jnp.int32, (128, 128), 0)
    columns = jnp.zeros((128, 128), F32)
    for g in range(n_gy):
        columns = jnp.where(lines == g, means[g], columns)
    columns = jnp.transpose(columns)
    for g in range(n_gy):
        r = slice(g * block, (g + 1) * block)
        for c in range(2):
            unit = (x_all[c, r, :].astype(F32) - columns[:block, g:g + 1]) * columns[block:2 * block, g:g + 1]
            nrm_all[c, r, :] = (unit * gains[c]).astype(BF16)
    prepare(pre, 0)
    reduce_step(pre, 0)
    if lag < far:
        prepare(hg, lag)
    prepare(pre, 1)
    if lag < far:
        reduce_step(hg, lag)
    reduce_step(pre, 1)

    def both(i):
        prepare(hg, lag + 1 + i)
        prepare(pre, 2 + i)
        reduce_step(hg, lag + 1 + i)
        reduce_step(pre, 2 + i)
    joint = max(far - lag - 1, 0)
    each(0, joint, both)

    def pre_step(s):
        prepare(pre, s)
        reduce_step(pre, s)
    prepare_end(hg)
    cut_in = min(2 + joint, far - 1)
    each(2 + joint, far - 1, pre_step)
    if far - 1 >= 2 + joint:
        prepare(pre, far - 1)
        cross_start(hg)
        reduce_step(pre, far - 1)
    else:
        cross_start(hg)
    prepare_end(pre)
    cross_start(pre)
    for i in range(early):
        hidden_grad = reduce_end(hg, i)
        hidden_pre = reduce_end(pre, i)
        phi = 0.5 * (1.0 + lax.erf(hidden_pre * 0.7071067811865476))
        slope = phi + hidden_pre * jnp.exp(-0.5 * hidden_pre * hidden_pre) * 0.3989422804014327
        at = slice(i * strip_cols, (i + 1) * strip_cols)
        full[0, core, rows_of(z), at] = (hidden_pre * phi).astype(BF16)
        full[1, core, rows_of(z), at] = (hidden_grad * slope).astype(BF16)

    strip = share // GSUBS
    pieces = [(w, k, g) for w in range(2) for g in range(GSUBS) for k in range(2)]
    own_pieces, other_pieces = pieces[:len(pieces) // 2], pieces[len(pieces) // 2:]

    def spread(piece, origin, ss, rs, row, neighbour, to_row):
        w, k, g = piece
        h = core if w == 0 else other
        name = h * (2 * GSUBS) + g * 2 + k
        ref = full.at[k, h, pl.ds(pl.multiple_of(origin * share + g * strip, strip), strip)]
        return remote(ref, ref, ss.at[row, name], rs.at[to_row, name], neighbour)

    def ring_send(s, piece):
        return spread(piece, behind(s), ga_ss, ga_rs, s, next_dev, s + 1)

    def ring_arrival(s, piece):
        return spread(piece, behind(s), ga_ss, ga_rs, 0, next_dev, s)

    def hand_over(piece, origin):
        return spread(piece, origin, gp_ss, gp_rs, origin, partner, origin)

    def process(origins, first, awaited):
        def join(ref, *index):
            parts = [ref[(*index, rows_of(o), slice(None))] for o in origins]
            return parts[0] if len(parts) == 1 else jnp.concatenate(parts, axis=0)

        def arrive():
            for o, some in awaited:
                for piece in some:
                    hand_over(piece, o).wait_recv()

        def products(k):
            weight, out, slots, ss, rs = ((w_out, br, br_in, br_ss, br_rs), (w_in, ng, ng_in, ng_ss, ng_rs))[k]
            product = dot(join(full, k, 0), weight[:, :half], 1, 1) + dot(join(full, k, 1), weight[:, half:], 1, 1)
            product = product.astype(BF16)
            for i, o in enumerate(origins):
                out[rows_of(o), :] = product[i * share:(i + 1) * share]

                @pl.when(o != gy)
                def _():
                    remote(out.at[rows_of(o)], slots.at[gy], ss.at[o], rs.at[gy], pdev(o)).start()

        def gradient(k):
            left, grad = ((up_all, grad_out), (nrm_all, grad_in))[k]
            lhs = join(left, core)
            for h in range(2):
                at = slice(h * half, (h + 1) * half)
                term = dot(lhs, join(full, k, h), 0, 0)
                grad[:, at] = term if first else grad[:, at] + term

        def begin():
            arrive()
            products(0)

        return begin, lambda: products(1), lambda: gradient(0), lambda: gradient(1)

    def gather_step(s, forward, work):
        for piece in pieces:
            ring_arrival(s, piece).wait_recv()
            if piece in forward:
                ring_send(s, piece).start()
            hand_over(piece, behind(s)).start()
        for part in work:
            part()

    for piece in own_pieces:
        ring_send(0, piece).start()
        hand_over(piece, z).start()
    for piece in other_pieces:
        hand_over(piece, z).wait_recv()
        ring_send(0, piece).start()

    def pairs(*steps):
        origins = sum(((behind(s), ahead(s)) for s in steps), ())
        return origins, False, tuple((ahead(s), pieces) for s in steps)

    todo = list(process((z,), True, ()))
    for s in range(1, far):
        if s >= 3 and s % 2 == 1:
            todo += process(*pairs(s - 2, s - 1))
        gather_step(s, pieces if s < far - 1 else own_pieces, todo[:2] if s < far - 1 else todo)
        todo = todo[2:] if s < far - 1 else []
    for work in process(*pairs(*((far - 1,) if far % 2 == 0 else (far - 2, far - 1)))):
        work()
    for piece in own_pieces:
        ring_arrival(far, piece).wait_recv()
        hand_over(piece, behind(far)).start()
    for work in process((behind(far),), False, ((behind(far), other_pieces),)):
        work()

    def rough(values):
        high = values.astype(BF16)
        return high, (values - high.astype(F32)).astype(BF16)

    ones_h = jnp.ones((8, half), BF16)
    lines = lax.broadcasted_iota(jnp.int32, (8, quarter), 0)
    packed = jnp.zeros((8, quarter), F32)
    lane_sums = []
    for k, grad in enumerate((grad_in, grad_out)):
        lane_sum = jnp.zeros((8, feats), F32)
        for h in range(2):
            values = grad[:, h * half:(h + 1) * half]
            sq = values * values + 1e-30
            high, low = rough(sq)
            lane_sum += dot(ones_h, high, 1, 1) + dot(ones_h, low, 1, 1)
            col = jnp.sum(sq, axis=0, keepdims=True)
            for q in range(2):
                packed = jnp.where(lines == 4 * k + 2 * h + q, col[:, q * quarter:(q + 1) * quarter], packed)
        lane_sums.append(lane_sum)
    col_m[...] = packed
    send_col = to_partner(col_m, col_p, 3)
    send_col.start()
    eight = lax.broadcasted_iota(jnp.int32, (8, feats), 0)
    lane1 = lax.broadcasted_iota(jnp.int32, (1, 128), 1)

    def total(values):
        return jnp.sum(values, axis=1, keepdims=True)

    def three(a, b, c):
        return jnp.where(lane1 == 0, a, jnp.where(lane1 == 1, b, c))

    sum_z[gx] = three(total(lane_sums[0][0:1]), total(lane_sums[1][0:1]), total(row_in[...]))
    sums_z = (sum_z, sz_ss, sz_rs)
    column_start(*sums_z)
    wide_feats = ph1.shape[1]
    message = jnp.where(eight == 0, lane_sums[0], lane_sums[1])
    if wide_feats > feats:
        message = jnp.concatenate([message, jnp.zeros((8, wide_feats - feats), F32)], axis=1)
    ph1[...] = message
    for k, g in enumerate(peers):
        remote(ph1, ph1_in.at[gy], p1_ss.at[k], p1_rs.at[gy], pdev(g)).start()

    send_col.wait()
    chip_cols = col_m[...] + col_p[...]
    col_h[...] = jnp.where(core == 0, chip_cols[:4], chip_cols[4:]).astype(BF16)
    chips_start(col_h, col_z, co_ss, co_rs)

    def scattered(out, slots, ss, rs):
        for g in peers:
            copy = remote(out.at[rows_of(g)], slots.at[g], ss.at[g], rs.at[g], pdev(g))
            copy.wait_send()
            copy.wait_recv()
        slots[gy] = out[own_block, :]
        return jnp.sum(slots[...].astype(F32), axis=0)

    scaled = scattered(ng, ng_in, ng_ss, ng_rs) * gain[...]
    unit = unit_s[...]
    message = across(jnp.sum(scaled, axis=1, keepdims=True), jnp.sum(scaled * unit, axis=1, keepdims=True))
    fin_z[gx] = message
    fin = (fin_z, fi_ss, fi_rs)
    column_start(*fin)
    output[...] = (patches[...].astype(F32) + scattered(br, br_in, br_ss, br_rs)).astype(BF16)
    for k, g in enumerate(peers):
        copy = remote(ph1, ph1_in.at[g], p1_ss.at[k], p1_rs.at[g], pdev(g))
        copy.wait_send()
        copy.wait_recv()
    ph1_in[gy] = ph1[...]
    sums = jnp.sum(ph1_in[...], axis=0)
    row_in_new = 0.9 * row_in[...] + 0.1 * (sums[0:1, :feats] / ff)
    col_out_new = 0.9 * col_out[...] + 0.1 * (sums[1:2, :feats] / ff)

    pair = jnp.where(
        lax.broadcasted_iota(jnp.int32, (128, feats), 0) == 0, lax.rsqrt(row_in_new), lax.rsqrt(col_out_new)
    )
    if wide_feats > feats:
        pair = jnp.concatenate([pair, jnp.zeros((128, wide_feats - feats), F32)], axis=1)
    turned = [jnp.transpose(pair[:, i * 128:(i + 1) * 128]) for i in range(wide_feats // 128)]
    factors = (turned[0] if len(turned) == 1 else jnp.concatenate(turned, axis=0))[:feats]

    column_wait(*sums_z)
    along = jnp.sum(sum_z[...], axis=0)
    old_rows = along[:, 2:3]
    sum_p[gy] = three(along[:, 0:1], along[:, 1:2], total(jnp.sum(row_out[...], axis=0, keepdims=True)))
    sums_p = (sum_p, sp_ss, sp_rs)
    small_start(*sums_p)
    chips_wait(col_h, col_z, co_ss, co_rs)
    col_z[z] = col_h[...]
    col_o[core] = jnp.sum(col_z[...].astype(F32), axis=0)
    send_out = to_partner(col_o.at[core], col_o.at[core], 4)
    send_out.start()
    reduce_sent(hg)
    reduce_sent(pre)

    def ring_sent(s, some):
        for piece in some:
            ring_send(s, piece).wait_send()
    each(0, far - 1, lambda s: ring_sent(s, pieces))
    ring_sent(far - 1, own_pieces)

    def handed_over(o, some):
        for piece in some:
            hand_over(piece, o).wait_send()
    handed_over(z, own_pieces)
    each(1, far, lambda s: handed_over(behind(s), pieces))
    handed_over(behind(far), own_pieces)
    send_out.wait_send()
    remote(col_o.at[core], col_o.at[other], pt_ss.at[4], pt_rs.at[4], partner).wait_recv()
    lines = quarter // 128
    for k, (grad, before) in enumerate(((grad_in, col_in), (grad_out, row_out))):
        column_sums = col_o[k] / d_model
        for q in range(4):
            at = slice(q * quarter, (q + 1) * quarter)
            old = [before[q * lines + i:q * lines + i + 1, :] for i in range(lines)]
            old = old[0] if lines == 1 else jnp.concatenate(old, axis=1)
            column = lax.rsqrt(0.9 * old + 0.1 * column_sums[q:q + 1])
            grad[:, at] = grad[:, at] * (factors[:, k:k + 1] * column)

    small_wait(*sums_p)
    everything_sum = jnp.sum(sum_p[...], axis=0)
    column_wait(*fin)
    final = jnp.sum(fin_z[...], axis=0)
    first_sum, second_sum = back(final)
    input_grad[...] = upstream[...].astype(F32) + inv_std * (
        scaled - first_sum / d_model - unit * (second_sum / d_model)
    )
    mean_in = (0.9 * old_rows + 0.1 * (everything_sum[:, 0:1] / ff)) / d_model
    mean_out = (0.9 * everything_sum[:, 2:3] + 0.1 * (everything_sum[:, 1:2] / d_model)) / ff
    which = lax.broadcasted_iota(jnp.int32, (8, 128), 0)
    totals[...] = jnp.sqrt(jnp.where(which == 0, mean_in, mean_out))


def exchange(n_gx, n_gy, d_model, args):
    patches, gain, upstream, w_in, w_out, row_in, col_out, col_in, row_out = args
    block, feats = patches.shape
    cols = w_in.shape[1]
    rows, half, nz = block * n_gy, cols // 2, n_gx // 2
    share, far = rows // nz, nz // 2
    quarter = half // 2
    wide_feats = -(-feats // 128) * 128
    pieces = 4 * GSUBS
    strips = cols // SUBS
    early = SUBS // 2
    vmem = pl.BlockSpec(memory_space=pltpu.VMEM)
    hbm = pl.BlockSpec(memory_space=pltpu.HBM)
    shapes = [(a.shape, a.dtype) for a in args] + [
        ((2, rows, feats), BF16), ((2, rows, feats), BF16), ((2, rows, feats), BF16),
        ((feats, cols), BF16), ((feats, cols), BF16), ((2, 1, feats), F32),
        ((share, cols), F32), ((share, cols), F32),
        ((far + 1, SUBS, share, strips), BF16), ((far + 1, SUBS, share, strips), BF16),
        ((early, share, strips), BF16), ((early, share, strips), BF16),
        ((2, 2, rows, half), BF16),
        ((block, feats), F32), ((n_gx, 1, 128), F32), ((n_gy, 1, 128), F32),
        ((rows, feats), BF16), ((rows, feats), BF16), ((n_gy, block, feats), BF16), ((n_gy, block, feats), BF16),
        ((8, wide_feats), F32), ((n_gy, 8, wide_feats), F32), ((n_gx, 1, 128), F32), ((n_gx, 1, 128), F32), ((n_gy, 1, 128), F32),
        ((8, quarter), F32), ((8, quarter), F32), ((4, quarter), BF16), ((nz, 4, quarter), BF16), ((2, 4, quarter), F32),
    ]
    counts = [(9,)] + [(n_gy,)] * 8 + [(6,)] * 2 + [(n_gx,)] * 6 + [(nz,)] * 2 + [(n_gy,)] * 2
    counts += [(n_gy,)] * 2 + [(far, SUBS), (far + 1, SUBS)] * 2 + [(early,)] * 4
    counts += [(far, pieces), (far + 1, pieces)] + [(nz, pieces)] * 2 + [(n_gy,)] * 6
    outs = [
        jax.ShapeDtypeStruct((block, feats), BF16), jax.ShapeDtypeStruct((block, feats), F32),
        jax.ShapeDtypeStruct((feats, cols), F32), jax.ShapeDtypeStruct((feats, cols), F32),
        jax.ShapeDtypeStruct((8, 128), F32),
    ]
    return pl.pallas_call(
        functools.partial(kernel, n_gx, n_gy, d_model),
        out_shape=outs,
        in_specs=[hbm] * 9,
        out_specs=[vmem] * 5,
        scratch_shapes=[pltpu.VMEM(s, t) for s, t in shapes] + [pltpu.SemaphoreType.DMA(c) for c in counts],
        compiler_params=pltpu.CompilerParams(
            collective_id=0, has_side_effects=True, vmem_limit_bytes=48 * 1024 * 1024
        ),
        name="block_step",
    )(*(pltpu.with_memory_space_constraint(a, pltpu.HBM) for a in args))


def finish_kernel(
    output, input_grad, grad_in, grad_out, totals, output_h, input_grad_h, update_in_h, update_out_h, new_in, new_out, sems
):
    small = [
        pltpu.make_async_copy(output, output_h, sems.at[0]), pltpu.make_async_copy(input_grad, input_grad_h, sems.at[1])
    ]
    for copy in small:
        copy.start()
    half = grad_in.shape[1] // 2
    copies = []
    for k, (grad, new, target) in enumerate(((grad_in, new_in, update_in_h), (grad_out, new_out, update_out_h))):
        for h in range(2):
            at = slice(h * half, (h + 1) * half)
            new[:, at] = grad[:, at] * totals[k:k + 1, 0:1]
            part = pl.ds(h * half, half)
            copy = pltpu.make_async_copy(new.at[:, part], target.at[:, part], sems.at[2 + 2 * k + h])
            copy.start()
            copies.append(copy)
    for copy in small + copies:
        copy.wait()


def finish(output, input_grad, grad_in, grad_out, totals):
    vmem = pl.BlockSpec(memory_space=pltpu.VMEM)
    hbm = pl.BlockSpec(memory_space=pltpu.HBM)
    arrays = (output, input_grad, grad_in, grad_out)
    return pl.pallas_call(
        finish_kernel,
        out_shape=[jax.ShapeDtypeStruct(a.shape, a.dtype) for a in arrays],
        in_specs=[vmem] * 5,
        out_specs=[hbm] * 4,
        scratch_shapes=[
            pltpu.VMEM(grad_in.shape, F32), pltpu.VMEM(grad_out.shape, F32), pltpu.SemaphoreType.DMA((6,))
        ],
        compiler_params=pltpu.CompilerParams(vmem_limit_bytes=16 * 1024 * 1024),
        name="scale_updates",
    )(*arrays, totals)


def solution(mesh):
    n_gx, n_gy = mesh.shape["gx"], mesh.shape["gy"]

    def body(patches, ln_gain, weight_in, weight_out, upstream, row_in, col_in, row_out, col_out):
        d_model = weight_in.shape[0] * n_gx
        results = exchange(
            n_gx, n_gy, d_model,
            (
                patches, ln_gain[None], upstream, weight_in, weight_out.T, row_in[None], col_out[None],
                col_in.reshape(-1, 128), row_out.reshape(-1, 128),
            ),
        )
        output, input_grad, update_in, update_out = finish(*results)
        return output, input_grad, update_in, update_out.T

    return jax.shard_map(
        body,
        mesh=mesh,
        in_specs=(
            P("gy", "gx"), P("gx"), P("gx", "gy"), P("gy", "gx"), P("gy", "gx"), P("gx"), P("gy"), P("gy"), P("gx"),
        ),
        out_specs=(P("gy", "gx"), P("gy", "gx"), P("gx", "gy"), P("gy", "gx")),
        check_vma=False,
    )
```

```python
import functools

import jax
import jax.numpy as jnp
from jax import lax
from jax.experimental import pallas as pl
from jax.experimental.pallas import tpu as pltpu
from jax.sharding import PartitionSpec as P

MESH = pl.DeviceIdType.MESH
F32 = jnp.float32
BF16 = jnp.bfloat16
SUBS = 4
GSUBS = 2
LAG = 2


def dot(a, b, ca, cb):
    return lax.dot_general(a, b, (((ca,), (cb,)), ((), ())), preferred_element_type=F32)


def aligned(i, n):
    return pl.multiple_of(i * n, n)


def plane_offsets(n_gy):
    side = next(k for k in range(int(n_gy ** 0.5), 0, -1) if n_gy % k == 0)
    wide = n_gy // side

    def hops(dy, dx):
        return min(dy, side - dy) + min(dx, wide - dx)

    offsets = [(dy, dx) for dy in range(side) for dx in range(wide) if dy or dx]
    return side, wide, sorted(offsets, key=lambda o: hops(*o))


def kernel(
    n_gx, n_gy, d_model,
    patches_h, gain_h, upstream_h, w_in_h, w_out_h, row_in_h, col_out_h, col_in_h, row_out_h,
    output, input_grad, grad_in, grad_out, totals,
    patches, gain, upstream, w_in, w_out, row_in, col_out, col_in, row_out,
    up_all, x_all, nrm_all, wo_p, wi_p, gains, hg_part, pre_part, hg_buf, pre_buf, hg_x, pre_x, full,
    unit_s, stat_z, means, br, ng, br_in, ng_in, ph1, ph1_in, fin_z, sum_z, sum_p,
    col_m, col_p, col_h, col_z, col_o,
    ld, up_ss, up_rs, uf_ss, uf_rs, xs_ss, xs_rs, xf_ss, xf_rs, pt_ss, pt_rs, st_ss, st_rs, fi_ss, fi_rs, sz_ss, sz_rs, co_ss, co_rs, sp_ss, sp_rs,
    ms_ss, ms_rs, hr_ss, hr_rs, pr_ss, pr_rs, hx_ss, hx_rs, px_ss, px_rs,
    ga_ss, ga_rs, gp_ss, gp_rs, br_ss, br_rs, ng_ss, ng_rs, p1_ss, p1_rs,
):
    gx = lax.axis_index("gx")
    gy = lax.axis_index("gy")
    nz = n_gx // 2
    z = lax.div(gx, 2)
    core = lax.rem(gx, 2)
    other = 1 - core
    block, feats = patches.shape
    rows = block * n_gy
    cols = w_in.shape[1]
    ff = cols * n_gy
    half = cols // 2
    quarter = half // 2
    share = rows // nz
    far = nz // 2
    side, wide, offsets = plane_offsets(n_gy)
    gy_y, gy_x = lax.div(gy, wide), lax.rem(gy, wide)
    peers = [lax.rem(gy_y + dy, side) * wide + lax.rem(gy_x + dx, wide) for dy, dx in offsets]

    def zdev(zz):
        return {"gx": zz * 2 + core, "gy": gy}

    def pdev(g):
        return {"gx": gx, "gy": g}

    partner = {"gx": z * 2 + other, "gy": gy}
    turn = 1 - 2 * core

    def ahead(k):
        return lax.rem(z + turn * k + nz, nz)

    def behind(k):
        return lax.rem(z - turn * k + nz, nz)

    next_dev = zdev(ahead(1))

    def remote(src, dst, ss, rs, dev):
        return pltpu.make_async_remote_copy(
            src_ref=src, dst_ref=dst, send_sem=ss, recv_sem=rs, device_id=dev, device_id_type=MESH
        )

    def each(lo, hi, f):
        def step(j, carry):
            f(j)
            return carry
        if lo < hi:
            lax.fori_loop(lo, hi, step, 0)

    loads = [
        pltpu.make_async_copy(a, b, ld.at[k]) for k, (a, b) in enumerate((
            (upstream_h, upstream), (patches_h, patches), (w_out_h, w_out), (w_in_h, w_in),
            (gain_h, gain), (row_in_h, row_in), (col_out_h, col_out),
            (col_in_h, col_in), (row_out_h, row_out),
        ))
    ]
    for copy in loads:
        copy.start()

    barrier = pltpu.get_barrier_semaphore()

    def greet(dev):
        pl.semaphore_signal(barrier, inc=1, device_id=dev, device_id_type=MESH)

    each(1, n_gx, lambda j: greet({"gx": lax.rem(gx + j, n_gx), "gy": gy}))
    for g in peers:
        greet(pdev(g))
    x_float = None
    loads[1].wait()

    def across(first, second):
        lane = lax.broadcasted_iota(jnp.int32, (block, 128), 1)
        parts = [jnp.where(lane == 0, first, 0.0), jnp.where(lane == 0, second, 0.0)]
        if 2 * block < 128:
            parts.append(jnp.zeros((128 - 2 * block, 128), F32))
        return jnp.transpose(jnp.concatenate(parts, axis=0))[:1]

    def back(message):
        tile = jnp.transpose(jnp.broadcast_to(message, (128, 128)))
        return tile[:block, 0:1], tile[block:2 * block, 0:1]

    x_float = patches[...].astype(F32)
    stat_z[gx] = across(
        jnp.sum(x_float, axis=1, keepdims=True), jnp.sum(x_float * x_float, axis=1, keepdims=True)
    )
    loads[0].wait()
    own_block = pl.ds(aligned(gy, block), block)
    up_all[core, own_block, :] = upstream[...]
    x_all[core, own_block, :] = patches[...]
    for copy in loads[2:]:
        copy.wait()
    gains[core] = gain[...]
    pl.semaphore_wait(barrier, n_gx - 1 + n_gy - 1)

    def to_partner(src, dst, k):
        return remote(src, dst, pt_ss.at[k], pt_rs.at[k], partner)

    def plane_start(src, everything, ss, rs, fs, fr):
        for k, g in enumerate(peers):
            remote(src, everything.at[core, own_block], ss.at[k], rs.at[gy], pdev(g)).start()
        remote(src, everything.at[core, own_block], fs.at[gy], fr.at[gy], partner).start()

    def plane_forward(src, everything, ss, rs, fs, fr):
        for k, g in enumerate(peers):
            landed = everything.at[core, pl.ds(aligned(g, block), block)]
            copy = remote(src, landed, ss.at[k], rs.at[g], pdev(g))
            copy.wait_recv()
            remote(landed, landed, fs.at[g], fr.at[g], partner).start()

    def plane_wait(src, everything, ss, rs, fs, fr):
        for k, g in enumerate(peers):
            remote(src, everything.at[core, own_block], ss.at[k], rs.at[g], pdev(g)).wait_send()

        def handed(g):
            landed = everything.at[other, pl.ds(aligned(g, block), block)]
            copy = remote(landed, landed, fs.at[g], fr.at[g], partner)
            copy.wait_send()
            copy.wait_recv()
        each(0, n_gy, handed)

    def chips_start(src, slots, ss, rs):
        def go(j):
            zz = lax.rem(z + j, nz)
            remote(src, slots.at[z], ss.at[j], rs.at[z], zdev(zz)).start()
        each(1, nz, go)

    def chips_wait(src, slots, ss, rs):
        def done(j):
            zz = lax.rem(z + j, nz)
            copy = remote(src, slots.at[zz], ss.at[j], rs.at[zz], zdev(zz))
            copy.wait_send()
            copy.wait_recv()
        each(1, nz, done)

    def column_copy(slots, ss, rs, j, source):
        return remote(slots.at[gx], slots.at[source], ss.at[j], rs.at[source], {"gx": lax.rem(gx + j, n_gx), "gy": gy})

    def column_start(slots, ss, rs):
        each(1, n_gx, lambda j: column_copy(slots, ss, rs, j, gx).start())

    def column_wait(slots, ss, rs):
        def done(j):
            copy = column_copy(slots, ss, rs, j, lax.rem(gx + j, n_gx))
            copy.wait_send()
            copy.wait_recv()
        each(1, n_gx, done)

    def small_copy(slots, ss, rs, k, source):
        return remote(slots.at[gy], slots.at[source], ss.at[k], rs.at[source], pdev(peers[k]))

    def small_start(slots, ss, rs):
        for k in range(len(peers)):
            small_copy(slots, ss, rs, k, gy).start()

    def small_wait(slots, ss, rs):
        for k, g in enumerate(peers):
            copy = small_copy(slots, ss, rs, k, g)
            copy.wait_send()
            copy.wait_recv()

    stat = (stat_z, st_ss, st_rs)
    column_start(*stat)
    up = (upstream, up_all, up_ss, up_rs, uf_ss, uf_rs)
    plane_start(*up)
    send_wo = to_partner(w_out, wo_p, 0)
    send_wo.start()
    xs = (patches, x_all, xs_ss, xs_rs, xf_ss, xf_rs)
    plane_start(*xs)
    send_wi = to_partner(w_in, wi_p, 1)
    send_wi.start()
    send_gain = to_partner(gains.at[core], gains.at[core], 5)
    send_gain.start()

    def rows_of(origin):
        return pl.ds(aligned(origin, share), share)

    def block_product(everything, own_weight, other_weight, t):
        r = rows_of(t)
        return dot(everything[core, r, :], own_weight, 1, 0) + dot(everything[other, r, :], other_weight, 1, 0)

    early = SUBS // 2
    strip_cols = cols // SUBS

    def sub_of(i):
        return lax.rem(i + core * early, SUBS)

    def prepare(kind, s):
        part, buf, ss, rs, everything, own_weight, other_weight, cross, xss, xrs = kind
        part[...] = block_product(everything, own_weight[...], other_weight[...], ahead(far - s))

    def reduce_step(kind, s):
        part, buf, ss, rs, everything, own_weight, other_weight, cross, xss, xrs = kind
        known = isinstance(s, int)
        for i in range(early if known and s == 0 else SUBS):
            sub = sub_of(i)
            own = part[:, pl.ds(pl.multiple_of(sub * strip_cols, 128), strip_cols)]
            here = buf.at[s, sub]
            if known and s == (0 if i < early else 1):
                buf[s, sub] = own.astype(BF16)
            else:
                remote(here, here, ss.at[s, sub], rs.at[s, sub], next_dev).wait_recv()
                buf[s, sub] = (buf[s, sub].astype(F32) + own).astype(BF16)
            remote(here, buf.at[s + 1, sub], ss.at[s, sub], rs.at[s + 1, sub], next_dev).start()

    def cross_copy(kind, i):
        part, buf, ss, rs, everything, own_weight, other_weight, cross, xss, xrs = kind
        return remote(buf.at[far, sub_of(early + i)], cross.at[i], xss.at[i], xrs.at[i], partner)

    def prepare_end(kind):
        part, buf, ss, rs, everything, own_weight, other_weight, cross, xss, xrs = kind
        mine = pl.ds(aligned(core, half), half)
        part[:, :half] = block_product(everything, own_weight[:, mine], other_weight[:, mine], z)

    def cross_start(kind):
        part, buf, ss, rs, everything, own_weight, other_weight, cross, xss, xrs = kind
        for i in range(early):
            sub = sub_of(early + i)
            remote(buf.at[far, sub], buf.at[far, sub], ss.at[0, sub], rs.at[far, sub], next_dev).wait_recv()
            cross_copy(kind, i).start()

    def reduce_end(kind, i):
        part, buf, ss, rs, everything, own_weight, other_weight, cross, xss, xrs = kind
        sub = sub_of(i)
        remote(buf.at[far, sub], buf.at[far, sub], ss.at[0, sub], rs.at[far, sub], next_dev).wait_recv()
        cross_copy(kind, i).wait_recv()
        own = part[:, i * strip_cols:(i + 1) * strip_cols]
        total = (own + buf[far, sub].astype(F32)) + cross[i].astype(F32)
        return total.astype(BF16).astype(F32)

    def reduce_sent(kind):
        part, buf, ss, rs, everything, own_weight, other_weight, cross, xss, xrs = kind

        def sent(s, count):
            for i in range(count):
                here = buf.at[s, sub_of(i)]
                remote(here, here, ss.at[s, sub_of(i)], rs.at[s, sub_of(i)], next_dev).wait_send()

        sent(0, early)
        each(1, far, lambda s: sent(s, SUBS))
        for i in range(early):
            cross_copy(kind, i).wait_send()

    hg = (hg_part, hg_buf, hr_ss, hr_rs, up_all, w_out, wo_p, hg_x, hx_ss, hx_rs)
    pre = (pre_part, pre_buf, pr_ss, pr_rs, nrm_all, w_in, wi_p, pre_x, px_ss, px_rs)

    column_wait(*stat)
    total, squares = back(jnp.sum(stat_z[...], axis=0))
    row_mean = total / d_model
    row_var = squares / d_model - row_mean * row_mean
    inv_std = lax.rsqrt(row_var + 1e-06)
    means[gy] = across(row_mean, inv_std)
    deviations = (means, ms_ss, ms_rs)
    small_start(*deviations)
    plane_forward(*up)
    plane_wait(*up)
    send_wo.wait()
    prepare(hg, 0)
    reduce_step(hg, 0)
    prepare(hg, 1)

    unit_s[...] = (patches[...].astype(F32) - row_mean) * inv_std
    plane_forward(*xs)
    reduce_step(hg, 1)
    lag = min(LAG, far)

    def hg_step(s):
        prepare(hg, s)
        reduce_step(hg, s)
    each(2, lag, hg_step)
    plane_wait(*xs)
    send_wi.wait()
    send_gain.wait_send()
    remote(gains.at[core], gains.at[other], pt_ss.at[5], pt_rs.at[5], partner).wait_recv()
    small_wait(*deviations)
    lines = lax.broadcasted_iota(jnp.int32, (128, 128), 0)
    columns = jnp.zeros((128, 128), F32)
    for g in range(n_gy):
        columns = jnp.where(lines == g, means[g], columns)
    columns = jnp.transpose(columns)
    for g in range(n_gy):
        r = slice(g * block, (g + 1) * block)
        for c in range(2):
            unit = (x_all[c, r, :].astype(F32) - columns[:block, g:g + 1]) * columns[block:2 * block, g:g + 1]
            nrm_all[c, r, :] = (unit * gains[c]).astype(BF16)
    prepare(pre, 0)
    reduce_step(pre, 0)
    if lag < far:
        prepare(hg, lag)
    prepare(pre, 1)
    if lag < far:
        reduce_step(hg, lag)
    reduce_step(pre, 1)

    def both(i):
        prepare(hg, lag + 1 + i)
        prepare(pre, 2 + i)
        reduce_step(hg, lag + 1 + i)
        reduce_step(pre, 2 + i)
    joint = max(far - lag - 1, 0)
    each(0, joint, both)

    def pre_step(s):
        prepare(pre, s)
        reduce_step(pre, s)
    prepare_end(hg)
    cut_in = min(2 + joint, far - 1)
    each(2 + joint, far - 1, pre_step)
    if far - 1 >= 2 + joint:
        prepare(pre, far - 1)
        cross_start(hg)
        reduce_step(pre, far - 1)
    else:
        cross_start(hg)
    prepare_end(pre)
    cross_start(pre)
    for i in range(early):
        hidden_grad = reduce_end(hg, i)
        hidden_pre = reduce_end(pre, i)
        phi = 0.5 * (1.0 + lax.erf(hidden_pre * 0.7071067811865476))
        slope = phi + hidden_pre * jnp.exp(-0.5 * hidden_pre * hidden_pre) * 0.3989422804014327
        at = slice(i * strip_cols, (i + 1) * strip_cols)
        full[0, core, rows_of(z), at] = (hidden_pre * phi).astype(BF16)
        full[1, core, rows_of(z), at] = (hidden_grad * slope).astype(BF16)

    strip = share // GSUBS
    pieces = [(w, k, g) for w in range(2) for g in range(GSUBS) for k in range(2)]
    own_pieces, other_pieces = pieces[:len(pieces) // 2], pieces[len(pieces) // 2:]

    def spread(piece, origin, ss, rs, row, neighbour, to_row):
        w, k, g = piece
        h = core if w == 0 else other
        name = h * (2 * GSUBS) + g * 2 + k
        ref = full.at[k, h, pl.ds(pl.multiple_of(origin * share + g * strip, strip), strip)]
        return remote(ref, ref, ss.at[row, name], rs.at[to_row, name], neighbour)

    def ring_send(s, piece):
        return spread(piece, behind(s), ga_ss, ga_rs, s, next_dev, s + 1)

    def ring_arrival(s, piece):
        return spread(piece, behind(s), ga_ss, ga_rs, 0, next_dev, s)

    def hand_over(piece, origin):
        return spread(piece, origin, gp_ss, gp_rs, origin, partner, origin)

    def process(origins, first, awaited):
        def join(ref, *index):
            parts = [ref[(*index, rows_of(o), slice(None))] for o in origins]
            return parts[0] if len(parts) == 1 else jnp.concatenate(parts, axis=0)

        def arrive():
            for o, some in awaited:
                for piece in some:
                    hand_over(piece, o).wait_recv()

        def products(k):
            weight, out, slots, ss, rs = ((w_out, br, br_in, br_ss, br_rs), (w_in, ng, ng_in, ng_ss, ng_rs))[k]
            product = dot(join(full, k, 0), weight[:, :half], 1, 1) + dot(join(full, k, 1), weight[:, half:], 1, 1)
            product = product.astype(BF16)
            for i, o in enumerate(origins):
                out[rows_of(o), :] = product[i * share:(i + 1) * share]

                @pl.when(o != gy)
                def _():
                    remote(out.at[rows_of(o)], slots.at[gy], ss.at[o], rs.at[gy], pdev(o)).start()

        def gradient(k):
            left, grad = ((up_all, grad_out), (nrm_all, grad_in))[k]
            lhs = join(left, core)
            for h in range(2):
                at = slice(h * half, (h + 1) * half)
                term = dot(lhs, join(full, k, h), 0, 0)
                grad[:, at] = term if first else grad[:, at] + term

        def begin():
            arrive()
            products(0)

        return begin, lambda: products(1), lambda: gradient(0), lambda: gradient(1)

    def gather_step(s, forward, work):
        for piece in pieces:
            ring_arrival(s, piece).wait_recv()
            if piece in forward:
                ring_send(s, piece).start()
            hand_over(piece, behind(s)).start()
        for part in work:
            part()

    for piece in own_pieces:
        ring_send(0, piece).start()
        hand_over(piece, z).start()
    for piece in other_pieces:
        hand_over(piece, z).wait_recv()
        ring_send(0, piece).start()

    def pairs(*steps):
        origins = sum(((behind(s), ahead(s)) for s in steps), ())
        return origins, False, tuple((ahead(s), pieces) for s in steps)

    todo = list(process((z,), True, ()))
    for s in range(1, far):
        if s >= 3 and s % 2 == 1:
            todo += process(*pairs(s - 2, s - 1))
        gather_step(s, pieces if s < far - 1 else own_pieces, todo[:2] if s < far - 1 else todo)
        todo = todo[2:] if s < far - 1 else []
    for work in process(*pairs(*((far - 1,) if far % 2 == 0 else (far - 2, far - 1)))):
        work()
    for piece in own_pieces:
        ring_arrival(far, piece).wait_recv()
        hand_over(piece, behind(far)).start()
    for work in process((behind(far),), False, ((behind(far), other_pieces),)):
        work()

    def rough(values):
        high = values.astype(BF16)
        return high, (values - high.astype(F32)).astype(BF16)

    def squares_of(k, h):
        values = (grad_in, grad_out)[k][:, h * half:(h + 1) * half]
        return values * values + 1e-30

    lane1 = lax.broadcasted_iota(jnp.int32, (1, 128), 1)

    def total(values):
        return jnp.sum(values, axis=1, keepdims=True)

    def three(a, b, c):
        return jnp.where(lane1 == 0, a, jnp.where(lane1 == 1, b, c))

    lines = lax.broadcasted_iota(jnp.int32, (8, quarter), 0)
    packed = jnp.zeros((8, quarter), F32)
    grand = []
    for k in range(2):
        grand.append(jnp.zeros((1, 1), F32))
        for h in range(2):
            col = jnp.sum(squares_of(k, h), axis=0, keepdims=True)
            grand[k] += total(col)
            for q in range(2):
                packed = jnp.where(lines == 4 * k + 2 * h + q, col[:, q * quarter:(q + 1) * quarter], packed)
    sum_z[gx] = three(grand[0], grand[1], total(row_in[...]))
    sums_z = (sum_z, sz_ss, sz_rs)
    column_start(*sums_z)
    col_m[...] = packed
    send_col = to_partner(col_m, col_p, 3)
    send_col.start()

    ones_h = jnp.ones((8, half), BF16)
    lane_sums = []
    for k in range(2):
        lane_sum = jnp.zeros((8, feats), F32)
        for h in range(2):
            high, low = rough(squares_of(k, h))
            lane_sum += dot(ones_h, high, 1, 1) + dot(ones_h, low, 1, 1)
        lane_sums.append(lane_sum)
    eight = lax.broadcasted_iota(jnp.int32, (8, feats), 0)
    wide_feats = ph1.shape[1]
    message = jnp.where(eight == 0, lane_sums[0], lane_sums[1])
    if wide_feats > feats:
        message = jnp.concatenate([message, jnp.zeros((8, wide_feats - feats), F32)], axis=1)
    ph1[...] = message
    for k, g in enumerate(peers):
        remote(ph1, ph1_in.at[gy], p1_ss.at[k], p1_rs.at[gy], pdev(g)).start()

    send_col.wait()
    chip_cols = col_m[...] + col_p[...]
    col_h[...] = jnp.where(core == 0, chip_cols[:4], chip_cols[4:]).astype(BF16)
    chips_start(col_h, col_z, co_ss, co_rs)

    def scattered(out, slots, ss, rs):
        for g in peers:
            copy = remote(out.at[rows_of(g)], slots.at[g], ss.at[g], rs.at[g], pdev(g))
            copy.wait_send()
            copy.wait_recv()
        slots[gy] = out[own_block, :]
        return jnp.sum(slots[...].astype(F32), axis=0)

    scaled = scattered(ng, ng_in, ng_ss, ng_rs) * gain[...]
    unit = unit_s[...]
    message = across(jnp.sum(scaled, axis=1, keepdims=True), jnp.sum(scaled * unit, axis=1, keepdims=True))
    fin_z[gx] = message
    fin = (fin_z, fi_ss, fi_rs)
    column_start(*fin)
    output[...] = (patches[...].astype(F32) + scattered(br, br_in, br_ss, br_rs)).astype(BF16)
    column_wait(*sums_z)
    along = jnp.sum(sum_z[...], axis=0)
    old_rows = along[:, 2:3]
    sum_p[gy] = three(along[:, 0:1], along[:, 1:2], total(jnp.sum(row_out[...], axis=0, keepdims=True)))
    sums_p = (sum_p, sp_ss, sp_rs)
    small_start(*sums_p)
    for k, g in enumerate(peers):
        copy = remote(ph1, ph1_in.at[g], p1_ss.at[k], p1_rs.at[g], pdev(g))
        copy.wait_send()
        copy.wait_recv()
    ph1_in[gy] = ph1[...]
    sums = jnp.sum(ph1_in[...], axis=0)
    row_in_new = 0.9 * row_in[...] + 0.1 * (sums[0:1, :feats] / ff)
    col_out_new = 0.9 * col_out[...] + 0.1 * (sums[1:2, :feats] / ff)

    pair = jnp.where(
        lax.broadcasted_iota(jnp.int32, (128, feats), 0) == 0, lax.rsqrt(row_in_new), lax.rsqrt(col_out_new)
    )
    if wide_feats > feats:
        pair = jnp.concatenate([pair, jnp.zeros((128, wide_feats - feats), F32)], axis=1)
    turned = [jnp.transpose(pair[:, i * 128:(i + 1) * 128]) for i in range(wide_feats // 128)]
    factors = (turned[0] if len(turned) == 1 else jnp.concatenate(turned, axis=0))[:feats]

    chips_wait(col_h, col_z, co_ss, co_rs)
    col_z[z] = col_h[...]
    col_o[core] = jnp.sum(col_z[...].astype(F32), axis=0)
    send_out = to_partner(col_o.at[core], col_o.at[core], 4)
    send_out.start()
    reduce_sent(hg)
    reduce_sent(pre)

    def ring_sent(s, some):
        for piece in some:
            ring_send(s, piece).wait_send()
    each(0, far - 1, lambda s: ring_sent(s, pieces))
    ring_sent(far - 1, own_pieces)

    def handed_over(o, some):
        for piece in some:
            hand_over(piece, o).wait_send()
    handed_over(z, own_pieces)
    each(1, far, lambda s: handed_over(behind(s), pieces))
    handed_over(behind(far), own_pieces)
    send_out.wait_send()
    remote(col_o.at[core], col_o.at[other], pt_ss.at[4], pt_rs.at[4], partner).wait_recv()
    lines = quarter // 128
    for k, (grad, before) in enumerate(((grad_in, col_in), (grad_out, row_out))):
        column_sums = col_o[k] / d_model
        for q in range(4):
            at = slice(q * quarter, (q + 1) * quarter)
            old = [before[q * lines + i:q * lines + i + 1, :] for i in range(lines)]
            old = old[0] if lines == 1 else jnp.concatenate(old, axis=1)
            column = lax.rsqrt(0.9 * old + 0.1 * column_sums[q:q + 1])
            grad[:, at] = grad[:, at] * (factors[:, k:k + 1] * column)

    small_wait(*sums_p)
    everything_sum = jnp.sum(sum_p[...], axis=0)
    column_wait(*fin)
    final = jnp.sum(fin_z[...], axis=0)
    first_sum, second_sum = back(final)
    input_grad[...] = upstream[...].astype(F32) + inv_std * (
        scaled - first_sum / d_model - unit * (second_sum / d_model)
    )
    mean_in = (0.9 * old_rows + 0.1 * (everything_sum[:, 0:1] / ff)) / d_model
    mean_out = (0.9 * everything_sum[:, 2:3] + 0.1 * (everything_sum[:, 1:2] / d_model)) / ff
    which = lax.broadcasted_iota(jnp.int32, (8, 128), 0)
    totals[...] = jnp.sqrt(jnp.where(which == 0, mean_in, mean_out))


def exchange(n_gx, n_gy, d_model, args):
    patches, gain, upstream, w_in, w_out, row_in, col_out, col_in, row_out = args
    block, feats = patches.shape
    cols = w_in.shape[1]
    rows, half, nz = block * n_gy, cols // 2, n_gx // 2
    share, far = rows // nz, nz // 2
    quarter = half // 2
    wide_feats = -(-feats // 128) * 128
    pieces = 4 * GSUBS
    strips = cols // SUBS
    early = SUBS // 2
    vmem = pl.BlockSpec(memory_space=pltpu.VMEM)
    hbm = pl.BlockSpec(memory_space=pltpu.HBM)
    shapes = [(a.shape, a.dtype) for a in args] + [
        ((2, rows, feats), BF16), ((2, rows, feats), BF16), ((2, rows, feats), BF16),
        ((feats, cols), BF16), ((feats, cols), BF16), ((2, 1, feats), F32),
        ((share, cols), F32), ((share, cols), F32),
        ((far + 1, SUBS, share, strips), BF16), ((far + 1, SUBS, share, strips), BF16),
        ((early, share, strips), BF16), ((early, share, strips), BF16),
        ((2, 2, rows, half), BF16),
        ((block, feats), F32), ((n_gx, 1, 128), F32), ((n_gy, 1, 128), F32),
        ((rows, feats), BF16), ((rows, feats), BF16), ((n_gy, block, feats), BF16), ((n_gy, block, feats), BF16),
        ((8, wide_feats), F32), ((n_gy, 8, wide_feats), F32), ((n_gx, 1, 128), F32), ((n_gx, 1, 128), F32), ((n_gy, 1, 128), F32),
        ((8, quarter), F32), ((8, quarter), F32), ((4, quarter), BF16), ((nz, 4, quarter), BF16), ((2, 4, quarter), F32),
    ]
    counts = [(9,)] + [(n_gy,)] * 8 + [(6,)] * 2 + [(n_gx,)] * 6 + [(nz,)] * 2 + [(n_gy,)] * 2
    counts += [(n_gy,)] * 2 + [(far, SUBS), (far + 1, SUBS)] * 2 + [(early,)] * 4
    counts += [(far, pieces), (far + 1, pieces)] + [(nz, pieces)] * 2 + [(n_gy,)] * 6
    outs = [
        jax.ShapeDtypeStruct((block, feats), BF16), jax.ShapeDtypeStruct((block, feats), F32),
        jax.ShapeDtypeStruct((feats, cols), F32), jax.ShapeDtypeStruct((feats, cols), F32),
        jax.ShapeDtypeStruct((8, 128), F32),
    ]
    return pl.pallas_call(
        functools.partial(kernel, n_gx, n_gy, d_model),
        out_shape=outs,
        in_specs=[hbm] * 9,
        out_specs=[vmem] * 5,
        scratch_shapes=[pltpu.VMEM(s, t) for s, t in shapes] + [pltpu.SemaphoreType.DMA(c) for c in counts],
        compiler_params=pltpu.CompilerParams(
            collective_id=0, has_side_effects=True, vmem_limit_bytes=48 * 1024 * 1024
        ),
        name="block_step",
    )(*(pltpu.with_memory_space_constraint(a, pltpu.HBM) for a in args))


def finish_kernel(
    output, input_grad, grad_in, grad_out, totals, output_h, input_grad_h, update_in_h, update_out_h, new_in, new_out, sems
):
    small = [
        pltpu.make_async_copy(output, output_h, sems.at[0]), pltpu.make_async_copy(input_grad, input_grad_h, sems.at[1])
    ]
    for copy in small:
        copy.start()
    half = grad_in.shape[1] // 2
    copies = []
    for k, (grad, new, target) in enumerate(((grad_in, new_in, update_in_h), (grad_out, new_out, update_out_h))):
        for h in range(2):
            at = slice(h * half, (h + 1) * half)
            new[:, at] = grad[:, at] * totals[k:k + 1, 0:1]
            part = pl.ds(h * half, half)
            copy = pltpu.make_async_copy(new.at[:, part], target.at[:, part], sems.at[2 + 2 * k + h])
            copy.start()
            copies.append(copy)
    for copy in small + copies:
        copy.wait()


def finish(output, input_grad, grad_in, grad_out, totals):
    vmem = pl.BlockSpec(memory_space=pltpu.VMEM)
    hbm = pl.BlockSpec(memory_space=pltpu.HBM)
    arrays = (output, input_grad, grad_in, grad_out)
    return pl.pallas_call(
        finish_kernel,
        out_shape=[jax.ShapeDtypeStruct(a.shape, a.dtype) for a in arrays],
        in_specs=[vmem] * 5,
        out_specs=[hbm] * 4,
        scratch_shapes=[
            pltpu.VMEM(grad_in.shape, F32), pltpu.VMEM(grad_out.shape, F32), pltpu.SemaphoreType.DMA((6,))
        ],
        compiler_params=pltpu.CompilerParams(vmem_limit_bytes=16 * 1024 * 1024),
        name="scale_updates",
    )(*arrays, totals)


def solution(mesh):
    n_gx, n_gy = mesh.shape["gx"], mesh.shape["gy"]

    def body(patches, ln_gain, weight_in, weight_out, upstream, row_in, col_in, row_out, col_out):
        d_model = weight_in.shape[0] * n_gx
        results = exchange(
            n_gx, n_gy, d_model,
            (
                patches, ln_gain[None], upstream, weight_in, weight_out.T, row_in[None], col_out[None],
                col_in.reshape(-1, 128), row_out.reshape(-1, 128),
            ),
        )
        output, input_grad, update_in, update_out = finish(*results)
        return output, input_grad, update_in, update_out.T

    return jax.shard_map(
        body,
        mesh=mesh,
        in_specs=(
            P("gy", "gx"), P("gx"), P("gx", "gy"), P("gy", "gx"), P("gy", "gx"), P("gx"), P("gy"), P("gy"), P("gx"),
        ),
        out_specs=(P("gy", "gx"), P("gy", "gx"), P("gx", "gy"), P("gy", "gx")),
        check_vma=False,
    )
```
